32 devices in a mesh: grp: 4 (over y, x), ep: 8 (over z, core).
Axes of the slice: x: 2, y: 2, z: 4, core: 2. Of those that a mesh axis runs over, the one named last changes fastest.
Arguments:
- token_ids: int32 [4, 8, 256], P('grp'), may hold values from 0 to 49215
- expert_routes: int32 [4, 8, 256, 8], P('grp', 'ep'), may hold values from 0 to 31, all different within a row; in each aligned block of 256 rows (0 to 255, 256 to 511, ..., all dimensions but the last counted through in order) at most 96 rows name the same one
- route_weights: float32 [4, 8, 256, 8], P('grp', 'ep'), may hold values from 0.2 to 0.8
- action_positions: int32 [4, 8, 32], P('grp', 'ep'), may hold values from 0 to 255
- action_tokens: int32 [4, 8, 32], P('grp'), may hold values from 0 to 49215
- advantages: float32 [4, 8, 32], P('grp'), may hold values from -5 to 5
- value_targets: float32 [4, 8, 32], P('grp', 'ep'), may hold values from -5 to 5
- owners: int32 [3843], replicated, may hold values from 0 to 3, as said below
- master_weights: float32 [7688, 8, 4096], P('grp', 'ep'), as said below
- first_moment: float32 [7688, 8, 4096], P('grp', 'ep'), as said below
- second_moment: float32 [7688, 8, 4096], P('grp', 'ep'), as said below
Outputs:
- loss: float32 [], replicated
- grad_norm: float32 [], replicated
- new_master: float32 [7688, 8, 4096], P('grp', 'ep')
- new_first: float32 [7688, 8, 4096], P('grp', 'ep')
- new_second: float32 [7688, 8, 4096], P('grp', 'ep')
The draws below stay inside these ranges and needn't reach their ends.
Inputs may be any that keep to these rules, and one draw needn't show every extreme that they name: `owners`: each index of grp owns at most 1922 blocks, and one owns exactly 1922. `expert_routes`: each token names 8 different experts; among the routes of one device's 256 tokens no expert is named more than 96 times, and some expert is named that often. `master_weights`: padding rows are zero; the attention part's blocks are equal in every column. `first_moment`: padding rows are zero; the attention part's blocks are equal in every column. `second_moment`: padding rows are zero, all others positive; the attention part's blocks are equal in every column.
All inputs are finite; a program needn't handle non-finite values.
Results may differ from the reference program's by a relative error of at most 0.014.
The reference program's roundings to bfloat16 on the way count: a program that leaves them out, or rounds other values in their place, can miss the bound.
Values may be sent and summed in bfloat16 or wider, within the bound.
No kernel may reach another device: no remote copies, remote signals or barrier semaphores. Data moves between devices by JAX's collectives and lax.ppermute only.
A program may use at most 576 MiB of HBM per device.

```python
import math
import jax
import jax.numpy as jnp
import numpy as np
from jax import lax

D = 1024
HEADS = 16
KV = 8
HD = 64
FF = 512
EXPERTS = 32
TOP = 8
VOCAB = 49216
BLK = 4096
ADAM_STEP = 10
SEQ_LEN = 256
ACT = 32
CAP_EXP = 96
EXP_DEV = 4
VS = 6152
SEQS = 32
NPOS = 1024
COL_NB = 3074
ATT_NB = 769
NB = 3843
CAP = 1922
N_GRP = 4
N_EP = 8


def owner_draw(key):
    key = jax.random.fold_in(key, 11)
    key_heavy, key_order, key_others = jax.random.split(key, 3)
    heavy = jax.random.randint(key_heavy, (), 0, N_GRP).astype(jnp.int32)
    order = jax.random.permutation(key_order, NB)
    others = jax.random.permutation(key_others, N_GRP - 1).astype(jnp.int32)
    remain = jnp.arange(NB, dtype=jnp.int32) - CAP
    half_size = (NB - CAP) // 2
    picked_idx = jnp.where(remain < half_size, remain % (N_GRP - 1), remain % (N_GRP // 2))
    offset = 1 + others[jnp.clip(picked_idx, 0, N_GRP - 2)]
    chosen = jnp.where(remain < 0, heavy, (heavy + offset) % N_GRP).astype(jnp.int32)
    return jnp.zeros((NB,), jnp.int32).at[order].set(chosen)


def row_blocks(owners):
    member = (owners[:, None] == jnp.arange(N_GRP, dtype=jnp.int32)[None, :]).astype(jnp.int32)
    ranking = jnp.sum((jnp.cumsum(member, axis=0) - member) * member, axis=1).astype(jnp.int32)
    return jnp.full((N_GRP * CAP,), NB, jnp.int32).at[owners * CAP + ranking].set(jnp.arange(NB, dtype=jnp.int32))


def lay_out(key, column_part, shared_part):
    stacked = jnp.concatenate([column_part, jnp.broadcast_to(shared_part[:, None, :], (ATT_NB, N_EP, BLK)), jnp.zeros((1, N_EP, BLK), jnp.float32)], axis=0)
    return stacked[row_blocks(owner_draw(key))]


def grad_unit():
    return CLIP_UNIT_BASE / math.sqrt(NPOS * (N_EP * COL_NB + ATT_NB) * BLK)


CLIP_UNIT_BASE = 24.0


TABLE_BASE = 0.8


HEAVY_SHARE = 0.0625


def column_positions():
    return jnp.arange(COL_NB, dtype=jnp.int32)[:, None] * BLK + jnp.arange(BLK, dtype=jnp.int32)[None, :]


def master_scales():
    col_pos = column_positions()
    gu_size = EXP_DEV * 2 * D * FF
    dn_size = EXP_DEV * FF * D
    col_scale = jnp.where(col_pos < gu_size, D ** (-0.5), jnp.where(col_pos < gu_size + dn_size, 2.0 * FF ** (-0.5), TABLE_BASE * D ** (-0.5)))
    att_pos = jnp.arange(ATT_NB, dtype=jnp.int32)[:, None] * BLK + jnp.arange(BLK, dtype=jnp.int32)[None, :]
    keyval_end = D * HEADS * HD + D * 2 * KV * HD
    out_end = keyval_end + HEADS * HD * D
    att_scale = jnp.where(att_pos < keyval_end, D ** (-0.5), jnp.where(att_pos < out_end, 3.0 * (HEADS * HD) ** (-0.5), D ** (-0.5)))
    is_gain = (att_pos >= out_end) & ((att_pos - out_end) // D < 3)
    return (col_scale, att_scale, is_gain)


def table_factors(key):
    col_pos = column_positions()
    offset = EXP_DEV * 2 * D * FF + EXP_DEV * FF * D
    row_pos = col_pos - offset
    is_table = row_pos >= 0
    row_index = jnp.clip(row_pos // D, 0, VS - 1).astype(jnp.int32)
    row_factor = jnp.exp(jax.random.uniform(key, (N_EP, VS), jnp.float32, -0.5, 1.0))
    spread = jnp.transpose(row_factor[:, row_index], (1, 0, 2))
    return jnp.where(is_table[:, None, :], spread, 1.0)


def draw_owners(key, part):
    return owner_draw(key)


def draw_master_weights(key, part):
    key_col, key_att, key_row = jax.random.split(jax.random.fold_in(key, 23), 3)
    col_scale, att_scale, is_gain = master_scales()
    column_part = jnp.clip(jax.random.normal(key_col, (COL_NB, N_EP, BLK), jnp.float32), -4.0, 4.0) * col_scale[:, None, :]
    column_part = column_part * table_factors(key_row)
    shared = jnp.clip(jax.random.normal(key_att, (ATT_NB, BLK), jnp.float32), -4.0, 4.0)
    shared = jnp.where(is_gain, 1.0 + 0.1 * shared, shared * att_scale)
    return lay_out(key, column_part, shared)


def draw_first_moment(key, part):
    key_col, key_att = jax.random.split(jax.random.fold_in(key, 37), 2)
    size = 0.11 * grad_unit()
    column_part = size * jnp.clip(jax.random.normal(key_col, (COL_NB, N_EP, BLK), jnp.float32), -4.0, 4.0)
    shared = size * jnp.clip(jax.random.normal(key_att, (ATT_NB, BLK), jnp.float32), -4.0, 4.0)
    return lay_out(key, column_part, shared)


def second_values(key, shape):
    key_base, key_tall, key_pick = jax.random.split(key, 3)
    base = jax.random.uniform(key_base, shape, jnp.float32, 0.3, 1.7)
    tall = jax.random.uniform(key_tall, shape, jnp.float32, 1000.0, 3000.0)
    pick = jax.random.uniform(key_pick, shape, jnp.float32, 0.0, 1.0) < HEAVY_SHARE
    return jnp.where(pick, tall, base)


def draw_second_moment(key, part):
    key_col, key_att = jax.random.split(jax.random.fold_in(key, 41), 2)
    size = 0.053 * grad_unit() * grad_unit()
    column_part = size * second_values(key_col, (COL_NB, N_EP, BLK))
    shared = size * second_values(key_att, (ATT_NB, BLK))
    return lay_out(key, column_part, shared)


def plant(array, own_key, smallest, top_value):
    dims = array.shape
    index_at = [jax.random.randint(jax.random.fold_in(own_key, axis), (), 0, dims[axis]) for axis in range(len(dims))]
    array = array.at[tuple(index_at)].set(smallest)
    longest = dims.index(max(dims))
    index_at[longest] = (index_at[longest] + 1) % dims[longest]
    return array.at[tuple(index_at)].set(top_value)


def block_levels(own_key, shape, cuts, least, high):
    factor_of = 1.0
    for position, parts in cuts:
        draws = jax.random.uniform(jax.random.fold_in(jax.random.fold_in(own_key, 6), position), (parts,), jnp.float32, least / len(cuts), high / len(cuts))
        factor_of = factor_of * jnp.repeat(jnp.exp(draws), shape[position] // parts).reshape((-1,) + (1,) * (len(shape) - 1 - position))
    return factor_of


def rank_table(number_of, slope):
    portions = [(1 << 20) // math.isqrt(grade ** slope) + 1 for grade in range(1, number_of + 1)]
    scale = 1 + sum(portions) // (1 << 30)
    return np.cumsum(np.array([max(1, weight // scale) for weight in portions]))


def skewed_ids(own_key, shape, count, skew):
    listing = rank_table(count, skew)
    ticket = jax.random.randint(jax.random.fold_in(own_key, 1), shape, 0, int(listing[count - 1]))
    standing = jnp.searchsorted(jnp.asarray(listing, jnp.int32), ticket, side="right")
    return jax.random.permutation(jax.random.fold_in(own_key, 2), count)[standing].astype(jnp.int32)


def shared_out(stream_key, own, number, rows, number_of, top, most, skew):
    order = jax.random.permutation(stream_key, number_of)
    packed, usual = portions_of(number_of, rows * top, most, skew, True), portions_of(number_of, rows * top, most, skew, False)
    places = jnp.arange(number_of)

    def named(sizes, offset_by):
        used = int((sizes > 0).sum())
        fixed = max(1, used // 4)
        passed = fixed + (places - fixed + offset_by * (used - fixed)) % max(1, number_of - fixed)
        return jnp.zeros((number_of,), jnp.int32).at[order[jnp.where(places < fixed, places, passed)]].set(jnp.asarray(sizes, jnp.int32))

    sizes = jnp.where(number % 4 == 0, named(packed, number // 4), named(usual, number - number // 4 - 1))
    mixed = jax.random.permutation(jax.random.fold_in(own, 3), number_of)
    donor, sink = mixed[0:number_of // 2 * 2:2], mixed[1:number_of // 2 * 2:2]
    room = jnp.minimum(sizes[donor] - 1, most - sizes[sink]) // 2
    room = jnp.where((donor == order[0]) | (sink == order[0]) | (sizes[sink] == 0), 0, jnp.maximum(room, 0))
    passed = jax.random.randint(jax.random.fold_in(own, 4), (number_of // 2,), 0, 1 << 20) % (room + 1)
    sizes = sizes.at[donor].add(-passed).at[sink].add(passed)
    items = jnp.searchsorted(jnp.cumsum(sizes), jnp.arange(rows * top), side="right").astype(jnp.int32)
    table = items.reshape(top, rows).T
    table = table[jax.random.permutation(jax.random.fold_in(own, 1), rows)]
    offset_by = jax.random.randint(jax.random.fold_in(own, 2), (rows, 1), 0, top)
    return jnp.take_along_axis(table, (jnp.arange(top)[None, :] + offset_by) % top, axis=1)


def portions_of(number_of, total, bound, lean, full):
    loads = [(1 << 20) // math.isqrt(standing ** lean) + 1 for standing in range(1, number_of + 1)]
    largest = bound if full else min(bound, max(-(-total // number_of), total * loads[0] // sum(loads)))
    least = 1 if total - largest >= number_of - 1 else 0
    holding, rest = [largest] + [least] * (number_of - 1), total - largest - least * (number_of - 1)
    while rest > 0:
        movable = [i for i in range(1, number_of) if holding[i] < largest] or [i for i in range(1, number_of) if holding[i] < bound]
        pool, remaining = sum([loads[i] for i in movable]), rest
        for i in movable:
            extra = min(bound - holding[i], max(1, remaining * loads[i] // pool), rest)
            holding[i] = holding[i] + extra
            rest = rest - extra
    return np.array(holding)


def normal_values(stream_key, dims, scale, limit, cuts=(), kind=jnp.bfloat16):
    array = jax.random.normal(stream_key, dims, jnp.float32) * scale
    if len(cuts) > 0:
        array = block_levels(stream_key, dims, cuts, -0.22, 0.18) * array
    return jnp.clip(array, min=-limit, max=limit).astype(kind)


def setup_inputs(seed: int = 0) -> dict:
    arg_keys = jax.random.split(jax.random.key(seed), 12)
    token_ids = plant(skewed_ids(arg_keys[0], (N_GRP, N_EP, SEQ_LEN), VOCAB, 2), jax.random.fold_in(arg_keys[0], 3), 0, VOCAB - 1).astype(jnp.int32)
    expert_routes_keys = jax.random.split(jax.random.fold_in(arg_keys[1], 1), N_GRP * N_EP * SEQ_LEN // SEQ_LEN)
    expert_routes_turns = jax.random.permutation(jax.random.fold_in(arg_keys[1], 3), N_GRP * N_EP * SEQ_LEN // SEQ_LEN)
    expert_routes = jax.vmap(lambda own, number: shared_out(jax.random.fold_in(arg_keys[1], 2), own, number, SEQ_LEN, EXPERTS, TOP, CAP_EXP, 1))(expert_routes_keys, expert_routes_turns).reshape((N_GRP, N_EP, SEQ_LEN, TOP))
    route_weights = jnp.clip(0.2 + 0.6 * jax.random.uniform(arg_keys[2], (N_GRP, N_EP, SEQ_LEN, TOP), jnp.float32) ** block_levels(arg_keys[2], (N_GRP, N_EP, SEQ_LEN, TOP), ((0, 4), (1, 8)), -0.2, 0.2), 0.2, 0.8)
    action_positions = plant(jax.random.randint(arg_keys[3], (N_GRP, N_EP, ACT), 0, SEQ_LEN), jax.random.fold_in(arg_keys[3], 1), 0, SEQ_LEN - 1).astype(jnp.int32)
    action_tokens = plant(jax.random.randint(arg_keys[4], (N_GRP, N_EP, ACT), 0, VOCAB), jax.random.fold_in(arg_keys[4], 1), 0, VOCAB - 1).astype(jnp.int32)
    advantages = normal_values(arg_keys[5], (N_GRP, N_EP, ACT), 1.0, 5.0, ((0, 4),), jnp.float32)
    value_targets = normal_values(arg_keys[6], (N_GRP, N_EP, ACT), 1.0, 5.0, ((0, 4), (1, 8)), jnp.float32)
    owners = draw_owners(jax.random.fold_in(arg_keys[11], 71), 0)
    master_weights = draw_master_weights(jax.random.fold_in(arg_keys[11], 71), 0)
    first_moment = draw_first_moment(jax.random.fold_in(arg_keys[11], 71), 0)
    second_moment = draw_second_moment(jax.random.fold_in(arg_keys[11], 71), 0)
    return {"token_ids": token_ids, "expert_routes": expert_routes, "route_weights": route_weights, "action_positions": action_positions, "action_tokens": action_tokens, "advantages": advantages, "value_targets": value_targets, "owners": owners, "master_weights": master_weights, "first_moment": first_moment, "second_moment": second_moment}


@jax.custom_vjp
def low(v):
    return lax.optimization_barrier(v.astype(jnp.bfloat16)).astype(jnp.float32)

@jax.custom_vjp
def low_back(v):
    return v

def low_keep(v):
    return (low(v), None)

def low_pass(kept, grad):
    return (grad,)

def back_keep(v):
    return (v, None)

def back_low(kept, grad):
    return (low(grad),)
low.defvjp(low_keep, low_pass)
low_back.defvjp(back_keep, back_low)
NORM_EPS = 1e-06
VALUE_COEF = 0.5
CLIP_BASE = 24.0
LEARN_RATE = 0.01
BETA_ONE = 0.9
BETA_TWO = 0.95
ADAM_EPS = 1e-08
WEIGHT_DECAY = 0.1
ROPE_BASE = 10000.0
MASK_FILL = -1e+30
HIGHEST = lax.Precision.HIGHEST

def rms_norm(values, gain_row):
    return values * lax.rsqrt(lax.optimization_barrier(jnp.mean(values * values, axis=-1, keepdims=True)) + NORM_EPS) * gain_row

def rope_tables(length):
    positions = jnp.arange(length).astype(jnp.float32)
    inverse = ROPE_BASE ** (-2.0 * jnp.arange(HD // 2).astype(jnp.float32) / HD)
    angles = positions[:, None] * inverse[None, :]
    return (jnp.cos(angles)[:, None, :], jnp.sin(angles)[:, None, :])

def rotate(values, cosine, sine_table):
    half_size = values.shape[-1] // 2
    front = values[..., :half_size]
    behind = values[..., half_size:]
    return jnp.concatenate([front * cosine - behind * sine_table, behind * cosine + front * sine_table], axis=-1)

def slot_tables(routes):
    flat_routes = routes.reshape(-1).astype(jnp.int32)
    pairs = flat_routes.shape[0]
    member = (flat_routes[:, None] == jnp.arange(EXPERTS, dtype=jnp.int32)[None, :]).astype(jnp.int32)
    ranking = lax.optimization_barrier(jnp.sum((jnp.cumsum(member, axis=0) - member) * member, axis=1)).astype(jnp.int32)
    pair_slot = (flat_routes * CAP_EXP + ranking).astype(jnp.int32)
    slot_pair = jnp.full((EXPERTS * CAP_EXP,), pairs, jnp.int32).at[pair_slot].set(jnp.arange(pairs, dtype=jnp.int32))
    return (pair_slot, slot_pair)

def column_rows(owners):
    member = (owners[:, None] == jnp.arange(N_GRP, dtype=jnp.int32)[None, :]).astype(jnp.int32)
    ranking = lax.optimization_barrier(jnp.sum((jnp.cumsum(member, axis=0) - member) * member, axis=1)).astype(jnp.int32)
    return (owners * CAP + ranking).astype(jnp.int32)

def split_attention(attention):
    query_end = D * HEADS * HD
    keyval_end = query_end + D * 2 * KV * HD
    out_end = keyval_end + HEADS * HD * D
    return (attention[:query_end].reshape(D, HEADS * HD), attention[query_end:keyval_end].reshape(D, 2 * KV * HD), attention[keyval_end:out_end].reshape(HEADS * HD, D), attention[out_end:].reshape(4, D))

def sequence_loss(weights, data):
    gate_up, down, table, w_query, w_keyval, w_out, gains = weights
    tokens, routes, mixing, places, actions, advantage, target = data
    length = tokens.shape[0]
    groups_per = HEADS // KV
    embed_scale = math.sqrt(D) / 2.0
    x_embed = embed_scale * low_back(table[tokens])
    normed = low(rms_norm(x_embed, gains[0]))
    query = low_back(jnp.dot(normed, w_query, precision=HIGHEST)).reshape(length, HEADS, HD)
    keyval = low_back(jnp.dot(normed, w_keyval, precision=HIGHEST)).reshape(length, 2, KV, HD)
    cosine, sine_table = rope_tables(length)
    query = low(rotate(query, cosine, sine_table)).reshape(length, KV, groups_per, HD)
    keys = low(rotate(keyval[:, 0], cosine, sine_table))
    values = low(keyval[:, 1])
    scores = low_back(jnp.einsum('tkgd,skd->kgts', query, keys, precision=HIGHEST) * HD ** (-0.5))
    causal = jnp.arange(length)[:, None] >= jnp.arange(length)[None, :]
    scores = jnp.where(causal, scores, MASK_FILL)
    probs = low(jax.nn.softmax(scores, axis=-1))
    attended = jnp.einsum('kgts,skd->tkgd', probs, values, precision=HIGHEST).reshape(length, HEADS * HD)
    attended = low(low_back(attended))
    x_attn = x_embed + low_back(jnp.dot(attended, w_out, precision=HIGHEST))
    mixed = low(rms_norm(x_attn, gains[1]))
    pair_slot, slot_pair = slot_tables(routes)
    copies = low_back(jnp.broadcast_to(mixed[:, None, :], (length, TOP, D))).reshape(length * TOP, D)
    padded = jnp.concatenate([copies, jnp.zeros((1, D), copies.dtype)], axis=0)
    slots = padded[slot_pair].reshape(EXPERTS, CAP_EXP, D)
    gate_val = low_back(jnp.einsum('ecd,edf->ecf', slots, gate_up, precision=HIGHEST))
    hidden = low(jax.nn.silu(gate_val[..., :FF]) * gate_val[..., FF:])
    expert_out = low(low_back(jnp.einsum('ecf,efd->ecd', hidden, down, precision=HIGHEST)))
    expert_out = expert_out.reshape(EXPERTS * CAP_EXP, D)
    chosen = expert_out[pair_slot].reshape(length, TOP, D)
    x_final = x_attn + lax.optimization_barrier(jnp.sum(mixing[:, :, None] * chosen, axis=1))
    final = rms_norm(x_final, gains[2])
    picked = final[places]
    value_pred = jnp.dot(picked, gains[3], precision=HIGHEST)
    logits = low_back(jnp.dot(low(picked), table.T, precision=HIGHEST))
    logp = jnp.take_along_axis(logits, actions[:, None], axis=1)[:, 0] - jax.nn.logsumexp(logits, axis=1)
    return jnp.sum(-advantage * logp + VALUE_COEF * (value_pred - target) ** 2) / NPOS

def reference(token_ids, expert_routes, route_weights, action_positions, action_tokens, advantages, value_targets, owners, master_weights, first_moment, second_moment):
    row_of_block = column_rows(owners)
    columns = jnp.transpose(master_weights[row_of_block], (1, 0, 2)).reshape(N_EP, NB * BLK)
    gu_size = EXP_DEV * D * 2 * FF
    dn_size = EXP_DEV * FF * D
    col_size = COL_NB * BLK
    gate_up = columns[:, :gu_size].reshape(EXPERTS, D, 2 * FF)
    down = columns[:, gu_size:gu_size + dn_size].reshape(EXPERTS, FF, D)
    table = columns[:, gu_size + dn_size:col_size].reshape(VOCAB, D)
    attention = columns[0, col_size:]
    data = (token_ids.reshape(SEQS, SEQ_LEN), expert_routes.reshape(SEQS, SEQ_LEN, TOP), route_weights.reshape(SEQS, SEQ_LEN, TOP), action_positions.reshape(SEQS, ACT), action_tokens.reshape(SEQS, ACT), advantages.reshape(SEQS, ACT), value_targets.reshape(SEQS, ACT))

    def total_loss(params):
        gu_full, dn_full, tab_full, att_full = params
        w_query, w_keyval, w_out, gains = split_attention(att_full)
        weights = tuple((low(item) for item in (gu_full, dn_full, tab_full, w_query, w_keyval, w_out, gains)))

        def advance(carry, item):
            return (carry + sequence_loss(weights, item), None)
        summed, _ = lax.scan(jax.checkpoint(advance), jnp.zeros((), jnp.float32), data)
        return summed
    loss, pullback = jax.vjp(total_loss, (gate_up, down, table, attention))
    (grad_gu, grad_dn, grad_tab, grad_att), = pullback(jnp.ones((), jnp.float32))
    square = jnp.sum(grad_gu * grad_gu) + jnp.sum(grad_dn * grad_dn) + jnp.sum(grad_tab * grad_tab) + jnp.sum(grad_att * grad_att)
    grad_norm = jnp.sqrt(square)
    factor = jnp.minimum(1.0, CLIP_BASE / math.sqrt(NPOS) / grad_norm)
    grad_cols = jnp.concatenate([grad_gu.reshape(N_EP, -1), grad_dn.reshape(N_EP, -1), grad_tab.reshape(N_EP, -1), jnp.broadcast_to(grad_att[None, :], (N_EP, grad_att.shape[0]))], axis=1).reshape(N_EP, NB, BLK)
    layout = jnp.zeros((N_GRP * CAP, N_EP, BLK), jnp.float32).at[row_of_block].set(jnp.transpose(grad_cols, (1, 0, 2)))
    valid = jnp.zeros((N_GRP * CAP,), bool).at[row_of_block].set(True)[:, None, None]
    clipped = factor * layout
    new_first = BETA_ONE * first_moment + (1.0 - BETA_ONE) * clipped
    new_second = BETA_TWO * second_moment + (1.0 - BETA_TWO) * clipped * clipped
    step_size = new_first / (1.0 - BETA_ONE ** ADAM_STEP) / (jnp.sqrt(new_second / (1.0 - BETA_TWO ** ADAM_STEP)) + ADAM_EPS)
    new_master = master_weights - LEARN_RATE * (step_size + WEIGHT_DECAY * master_weights)
    return (loss, grad_norm, jnp.where(valid, new_master, 0.0), jnp.where(valid, new_first, 0.0), jnp.where(valid, new_second, 0.0))
```

```python
import functools
import math

import jax
import jax.numpy as jnp
from jax import lax
from jax.experimental import pallas as pl
from jax.experimental.pallas import tpu as pltpu
from jax.sharding import PartitionSpec as P

D = 1024
HEADS = 16
KV = 8
HD = 64
FF = 512
EXPERTS = 32
TOP = 8
VOCAB = 49216
ADAM_STEP = 10
CAP_EXP = 96


NORM_EPS = 1e-06
VALUE_COEF = 0.5
CLIP_BASE = 24.0
LEARN_RATE = 0.01
BETA_ONE = 0.9
BETA_TWO = 0.95
ADAM_EPS = 1e-08
WEIGHT_DECAY = 0.1
ROPE_BASE = 10000.0
MASK_FILL = -1e30
LANES = 128
CHUNK = 64
BATCH = 64


def combined_all(value, axis, combine):
    everything = jax.tree.map(lambda part: lax.all_gather(part, axis), value)
    initial = jax.tree.map(lambda part: part[0], everything)

    def turn(k, so_far):
        return combine(so_far, jax.tree.map(lambda part: part[k], everything))

    return lax.fori_loop(1, lax.axis_size(axis), turn, initial)


def rms_norm(values, gain_row):
    return (
        values * lax.rsqrt(jnp.mean(values * values, axis=-1, keepdims=True) + NORM_EPS) * gain_row
    )


def rope_tables(length):
    positions = jnp.arange(length).astype(jnp.float32)
    inverse = ROPE_BASE ** (-2.0 * jnp.arange(HD // 2).astype(jnp.float32) / HD)
    angles = positions[:, None] * inverse[None, :]
    return (jnp.cos(angles)[:, None, :], jnp.sin(angles)[:, None, :])


def rotate(values, cosine, sine_table):
    half_size = values.shape[-1] // 2
    front = values[..., :half_size]
    behind = values[..., half_size:]
    return jnp.concatenate(
        [front * cosine - behind * sine_table, behind * cosine + front * sine_table], axis=-1
    )


def rotate_back(values, cosine, sine_table):
    half_size = values.shape[-1] // 2
    front = values[..., :half_size]
    behind = values[..., half_size:]
    return jnp.concatenate(
        [front * cosine + behind * sine_table, behind * cosine - front * sine_table], axis=-1
    )


def slot_tables(routes):
    flat_routes = routes.reshape(-1)
    pairs = flat_routes.shape[0]
    member = (flat_routes[:, None] == jnp.arange(EXPERTS, dtype=jnp.int32)[None, :]).astype(
        jnp.int32
    )
    ranking = jnp.sum((jnp.cumsum(member, axis=0) - member) * member, axis=1)
    pair_slot = flat_routes * CAP_EXP + ranking
    slot_pair = (
        jnp.full((EXPERTS * CAP_EXP,), pairs, jnp.int32)
        .at[pair_slot]
        .set(jnp.arange(pairs, dtype=jnp.int32))
    )
    return (pair_slot, slot_pair)


def ring_order(count):
    side = math.isqrt(count)
    if side * side != count or side % 2:
        return list(range(count))
    path = []
    for y in range(side):
        row = range(1, side) if y % 2 == 0 else range(side - 1, 0, -1)
        path += [y * side + x for x in row]
    path += [y * side for y in range(side - 1, -1, -1)]
    return path


def cast_kernel(src_ref, out_ref):
    out_ref[...] = src_ref[...].astype(jnp.bfloat16)


def cast_rows(rows, extra):
    count, sub, _ = rows.shape
    return pl.pallas_call(
        cast_kernel,
        out_shape=jax.ShapeDtypeStruct((count + extra, sub, LANES), jnp.bfloat16),
        grid=(pl.cdiv(count, BATCH),),
        in_specs=[pl.BlockSpec((BATCH, sub, LANES), lambda i: (i, 0, 0))],
        out_specs=pl.BlockSpec((BATCH, sub, LANES), lambda i: (i, 0, 0)),
        name="cast_rows",
    )(rows)


def fetch_blocks(idx_ref, first_ref, second_ref, buf, sem, step, slot):
    limit = first_ref.shape[0]

    def body(k, carry):
        b = idx_ref[step * BATCH + k]

        @pl.when(b < limit)
        def _():
            pltpu.make_async_copy(first_ref.at[b], buf.at[slot, k], sem.at[slot]).start()

        @pl.when(b >= limit)
        def _():
            pltpu.make_async_copy(second_ref.at[b - limit], buf.at[slot, k], sem.at[slot]).start()

        return carry

    lax.fori_loop(0, BATCH, body, 0, unroll=8)


def unpack_kernel(idx_ref, first_ref, second_ref, out_ref, buf, wide, sem):
    i = pl.program_id(0)
    slot = lax.rem(i, 2)

    @pl.when(i == 0)
    def _():
        fetch_blocks(idx_ref, first_ref, second_ref, buf, sem, 0, 0)

    @pl.when(i + 1 < pl.num_programs(0))
    def _():
        fetch_blocks(idx_ref, first_ref, second_ref, buf, sem, i + 1, 1 - slot)

    pltpu.make_async_copy(first_ref.at[pl.ds(0, BATCH)], buf.at[slot], sem.at[slot]).wait()
    sub = buf.shape[2]
    per = D // LANES
    wide[...] = buf[slot].astype(jnp.float32).reshape(BATCH * sub, LANES)
    for j in range(per):
        out_ref[:, LANES * j : LANES * (j + 1)] = wide[
            pl.ds(j, BATCH * sub // per, stride=per), :
        ].astype(jnp.bfloat16)


def pad_index(index):
    count = index.shape[0]
    return jnp.pad(index, (0, pl.cdiv(count, BATCH) * BATCH - count)).astype(jnp.int32)


def unpack(streams, index):
    first, second = streams
    count = index.shape[0]
    sub = first.shape[1]
    rows = sub * LANES // D
    return pl.pallas_call(
        unpack_kernel,
        out_shape=jax.ShapeDtypeStruct((count * rows, D), jnp.bfloat16),
        grid_spec=pltpu.PrefetchScalarGridSpec(
            num_scalar_prefetch=1,
            grid=(pl.cdiv(count, BATCH),),
            in_specs=[pl.BlockSpec(memory_space=pl.ANY), pl.BlockSpec(memory_space=pl.ANY)],
            out_specs=pl.BlockSpec((BATCH * rows, D), lambda i, idx: (i, 0)),
            scratch_shapes=[
                pltpu.VMEM((2, BATCH, sub, LANES), jnp.bfloat16),
                pltpu.VMEM((BATCH * sub, LANES), jnp.float32),
                pltpu.SemaphoreType.DMA((2,)),
            ],
        ),
        cost_estimate=pl.CostEstimate(
            flops=0, bytes_accessed=4 * count * sub * LANES, transcendentals=0
        ),
        name="unpack",
    )(pad_index(index), first, second)


def own_kernel(idx_ref, first_ref, second_ref, out_ref, buf, sem):
    i = pl.program_id(0)
    slot = lax.rem(i, 2)

    @pl.when(i == 0)
    def _():
        fetch_blocks(idx_ref, first_ref, second_ref, buf, sem, 0, 0)

    @pl.when(i + 1 < pl.num_programs(0))
    def _():
        fetch_blocks(idx_ref, first_ref, second_ref, buf, sem, i + 1, 1 - slot)

    pltpu.make_async_copy(first_ref.at[pl.ds(0, BATCH)], buf.at[slot], sem.at[slot]).wait()
    out_ref[...] = buf[slot]


def take_blocks(streams, index):
    first, second = streams
    count = index.shape[0]
    sub = first.shape[1]
    return pl.pallas_call(
        own_kernel,
        out_shape=jax.ShapeDtypeStruct((count, sub, LANES), jnp.bfloat16),
        grid_spec=pltpu.PrefetchScalarGridSpec(
            num_scalar_prefetch=1,
            grid=(pl.cdiv(count, BATCH),),
            in_specs=[pl.BlockSpec(memory_space=pl.ANY), pl.BlockSpec(memory_space=pl.ANY)],
            out_specs=pl.BlockSpec((BATCH, sub, LANES), lambda i, idx: (i, 0, 0)),
            scratch_shapes=[
                pltpu.VMEM((2, BATCH, sub, LANES), jnp.bfloat16),
                pltpu.SemaphoreType.DMA((2,)),
            ],
        ),
        name="take_blocks",
    )(pad_index(index), first, second)


def pack_kernel(count, keep, idx_ref, src_ref, *refs):
    first_ref, second_ref, wide, buf, sem = refs[2:] if keep else refs
    i = pl.program_id(0)
    steps = pl.num_programs(0)
    slot = lax.rem(i, 2)
    limit = first_ref.shape[0]
    sub = buf.shape[2]
    per = D // LANES
    last = count - (pl.cdiv(count, BATCH) - 1) * BATCH

    def drain(which, blocks):
        pltpu.make_async_copy(
            buf.at[which, pl.ds(0, blocks)], first_ref.at[pl.ds(0, blocks)], sem.at[which]
        ).wait()

    @pl.when(i >= 2)
    def _():
        drain(slot, BATCH)

    for j in range(per):
        wide[pl.ds(j, BATCH * sub // per, stride=per), :] = src_ref[
            :, LANES * j : LANES * (j + 1)
        ].astype(jnp.float32)
    buf[slot] = wide[...].reshape(BATCH, sub, LANES).astype(jnp.bfloat16)

    def body(k, carry):
        b = idx_ref[i * BATCH + k]

        @pl.when(b < limit)
        def _():
            pltpu.make_async_copy(buf.at[slot, k], first_ref.at[b], sem.at[slot]).start()

        @pl.when(b >= limit)
        def _():
            pltpu.make_async_copy(buf.at[slot, k], second_ref.at[b - limit], sem.at[slot]).start()

        return carry

    @pl.when(i < steps - 1)
    def _():
        lax.fori_loop(0, BATCH, body, 0, unroll=8)

    @pl.when(i == steps - 1)
    def _():
        lax.fori_loop(0, last, body, 0)
        drain(slot, last)

        @pl.when(i >= 1)
        def _():
            drain(1 - slot, BATCH)


def pack(grad, index, size, streams=None):
    count = index.shape[0]
    rows = grad.shape[0] // count
    sub = rows * D // LANES
    keep = streams is not None
    shape = jax.ShapeDtypeStruct((size, sub, LANES), jnp.bfloat16)
    anywhere = pl.BlockSpec(memory_space=pl.ANY)
    return pl.pallas_call(
        functools.partial(pack_kernel, count, keep),
        out_shape=(shape, shape),
        grid_spec=pltpu.PrefetchScalarGridSpec(
            num_scalar_prefetch=1,
            grid=(pl.cdiv(count, BATCH),),
            in_specs=[pl.BlockSpec((BATCH * rows, D), lambda i, idx: (i, 0))]
            + ([anywhere, anywhere] if keep else []),
            out_specs=(anywhere, anywhere),
            scratch_shapes=[
                pltpu.VMEM((BATCH * sub, LANES), jnp.float32),
                pltpu.VMEM((2, BATCH, sub, LANES), jnp.bfloat16),
                pltpu.SemaphoreType.DMA((2,)),
            ],
        ),
        input_output_aliases={2: 0, 3: 1} if keep else {},
        cost_estimate=pl.CostEstimate(
            flops=0, bytes_accessed=6 * count * sub * LANES, transcendentals=0
        ),
        name="pack",
    )(pad_index(index), grad, *(streams if keep else ()))


def update_kernel(scal_ref, count_ref, grad_ref, m_ref, f_ref, s_ref, om_ref, of_ref, os_ref):
    i = pl.program_id(0)
    rows = grad_ref.shape[0]
    row = i * rows + lax.broadcasted_iota(jnp.int32, grad_ref.shape, 0)
    keep = row < count_ref[0]
    clipped = scal_ref[0] * grad_ref[...].astype(jnp.float32)
    master = m_ref[...]
    new_first = BETA_ONE * f_ref[...] + (1.0 - BETA_ONE) * clipped
    new_second = BETA_TWO * s_ref[...] + (1.0 - BETA_TWO) * clipped * clipped
    step_size = (
        new_first
        / (1.0 - BETA_ONE**ADAM_STEP)
        / (jnp.sqrt(new_second / (1.0 - BETA_TWO**ADAM_STEP)) + ADAM_EPS)
    )
    new_master = master - LEARN_RATE * (step_size + WEIGHT_DECAY * master)
    om_ref[...] = jnp.where(keep, new_master, 0.0)
    of_ref[...] = jnp.where(keep, new_first, 0.0)
    os_ref[...] = jnp.where(keep, new_second, 0.0)


def update(factor, valid, grad, master, first, second):
    count, sub, _ = grad.shape
    tile = next(t for t in range(64, 0, -1) if count % t == 0)
    spec = pl.BlockSpec((tile, sub, LANES), lambda i, a, b: (i, 0, 0))
    shape = jax.ShapeDtypeStruct(grad.shape, jnp.float32)
    return pl.pallas_call(
        update_kernel,
        out_shape=(shape, shape, shape),
        grid_spec=pltpu.PrefetchScalarGridSpec(
            num_scalar_prefetch=2,
            grid=(count // tile,),
            in_specs=[spec] * 4,
            out_specs=(spec, spec, spec),
        ),
        name="update",
    )(factor.reshape(1), valid.reshape(1), grad, master, first, second)


class Part:
    def __init__(self, lo, hi, member, before, counts_before, ring_pos, my_pos):
        groups = member.shape[1]
        self.lo, self.count, self.groups = lo, hi - lo, groups
        self.size = (hi - lo) // 2 + groups + (groups + 1) * CHUNK
        inside = member[lo:hi]
        self.held = jnp.sum(inside, axis=0)
        self.base = counts_before
        rank = jnp.sum((before[lo:hi] - counts_before[None, :]) * inside, axis=1)
        half = (self.held + 1) // 2
        halves = (half, self.held - half)
        self.half = half
        self.steps = []
        self.gather_seg, self.scatter_seg, self.lag, self.scatter_lag = [], [], [], []
        padded_sum = []
        steps = jnp.zeros((), jnp.int32)
        slots = jnp.arange(groups, dtype=jnp.int32)
        for way in (0, 1):
            wide = jnp.maximum(halves[way], CHUNK)
            at_ring = jnp.sum(jnp.where(ring_pos[None, :] == slots[:, None], wide[None, :], 0), axis=1)
            steps = jnp.maximum(steps, jnp.max(jnp.sum(at_ring) - at_ring))
            turn = 1 if way == 0 else -1

            def starts(origin):
                gap = ((origin - slots) * turn) % groups
                earlier = gap[None, :] < gap[:, None]
                return jnp.sum(jnp.where(earlier, at_ring[None, :], 0), axis=1)

            def by_group(ring_values):
                return jnp.sum(
                    jnp.where(ring_pos[:, None] == slots[None, :], ring_values[None, :], 0), axis=1
                )

            here = jnp.sum(jnp.where(slots == my_pos, at_ring, 0))
            prev = jnp.sum(jnp.where(slots == (my_pos - turn) % groups, at_ring, 0))
            self.lag.append(here)
            self.scatter_lag.append(prev)
            self.gather_seg.append(by_group(starts(my_pos)))
            self.scatter_seg.append(by_group(starts((my_pos - turn) % groups)))
        self.dyn_steps = (steps + CHUNK - 1) // CHUNK
        self.fixed_steps = int(0.45 * (hi - lo)) // CHUNK

        def place(seg):
            up = jnp.sum((seg[0])[None, :] * inside, axis=1) + rank
            down = jnp.sum((seg[1] - half)[None, :] * inside, axis=1) + rank + self.size
            return jnp.where(rank < jnp.sum(half[None, :] * inside, axis=1), up, down)

        self.gather_place = place(self.gather_seg)
        self.scatter_place = place(self.scatter_seg)


def ring_links(count):
    order = ring_order(count)
    up = [(order[k], order[(k + 1) % count]) for k in range(count)]
    return up, [(b, a) for a, b in up]


def pick(vector, index):
    return jnp.sum(jnp.where(jnp.arange(vector.shape[0]) == index, vector, 0))


def run_ring(part, streams, step):
    for s in range(part.fixed_steps):
        streams = [step(s, way, streams[way]) for way in (0, 1)]

    def body(s, carry):
        return tuple(step(s, way, carry[way]) for way in (0, 1))

    return lax.fori_loop(part.fixed_steps, part.dyn_steps, body, tuple(streams))


def ring_gather(part, own, group_index):
    links = ring_links(part.groups)
    base = pick(part.base, group_index)
    half = pick(part.half, group_index)
    streams = [
        lax.dynamic_slice_in_dim(own, start, part.size) for start in (base, base + half)
    ]

    def step(s, way, stream):
        sent = lax.dynamic_slice_in_dim(stream, s * CHUNK, CHUNK)
        got = lax.ppermute(sent, "grp", links[way])
        at = jnp.minimum(part.lag[way] + s * CHUNK, part.size - CHUNK)
        return lax.dynamic_update_slice_in_dim(stream, got, at, 0)

    return run_ring(part, streams, step)


def ring_scatter(part, streams):
    links = ring_links(part.groups)

    def step(s, way, stream):
        sent = lax.dynamic_slice_in_dim(stream, s * CHUNK, CHUNK)
        got = lax.ppermute(sent, "grp", links[way])
        at = jnp.minimum(part.scatter_lag[way] + s * CHUNK, part.size - CHUNK)
        old = lax.dynamic_slice_in_dim(stream, at, CHUNK)
        total = (old.astype(jnp.float32) + got.astype(jnp.float32)).astype(jnp.bfloat16)
        return lax.dynamic_update_slice_in_dim(stream, total, at, 0)

    return run_ring(part, streams, step)


def own_index(part, group_index, row, offset):
    k = row - pick(part.base, group_index)
    half = pick(part.half, group_index)
    up = pick(part.scatter_seg[0], group_index) + k
    down = pick(part.scatter_seg[1], group_index) + k - half + part.size
    inside = (k >= 0) & (k < pick(part.held, group_index))
    return inside, jnp.where(k < half, up, down) + offset


def combine_stats(earlier, later):
    top_score = jnp.maximum(earlier[0], later[0])
    mass = earlier[1] * jnp.exp(earlier[0] - top_score) + later[1] * jnp.exp(later[0] - top_score)
    return (top_score, mass, earlier[2] + later[2])


def on_device(
    token_ids,
    expert_routes,
    route_weights,
    action_positions,
    action_tokens,
    advantages,
    value_targets,
    owners,
    master_weights,
    first_moment,
    second_moment,
):
    groups = lax.axis_size("grp")
    shards = lax.axis_size("ep")
    group_index = lax.axis_index("grp")
    shard_index = lax.axis_index("ep")
    capacity = master_weights.shape[0]
    row_width = master_weights.shape[2]
    blocks = owners.shape[0]
    length = token_ids.shape[2]
    act_count = action_positions.shape[2]
    local_experts = EXPERTS // shards
    vocab_rows = VOCAB // shards
    npos = groups * shards * act_count
    groups_per = HEADS // KV
    embed_scale = math.sqrt(D) / 2.0
    gu_size = local_experts * D * 2 * FF
    dn_size = local_experts * FF * D
    col_size = gu_size + dn_size + vocab_rows * D
    query_end = col_size + D * HEADS * HD
    keyval_end = query_end + D * 2 * KV * HD
    out_end = keyval_end + HEADS * HD * D
    sub = row_width // LANES
    order = ring_order(groups)
    ring_pos = jnp.array([order.index(g) for g in range(groups)], jnp.int32)
    my_pos = pick(ring_pos, group_index)
    member = (owners[:, None] == jnp.arange(groups, dtype=jnp.int32)[None, :]).astype(jnp.int32)
    before = jnp.cumsum(member, axis=0) - member
    marks = [0, (gu_size + dn_size) // row_width, col_size // row_width, blocks]
    parts = []
    counts_before = jnp.zeros((groups,), jnp.int32)
    for lo, hi in zip(marks[:-1], marks[1:]):
        parts.append(Part(lo, hi, member, before, counts_before, ring_pos, my_pos))
        counts_before = counts_before + parts[-1].held
    exp_part, tab_part, att_part = parts
    master_rows = master_weights.reshape(capacity, sub, LANES)
    own = cast_rows(master_rows, max(part.size for part in parts))
    tab_streams = ring_gather(tab_part, own, group_index)
    own, tab_streams = lax.optimization_barrier((own, tab_streams))
    table = unpack(tab_streams, tab_part.gather_place)
    att_streams = ring_gather(att_part, own, group_index)
    own, att_streams = lax.optimization_barrier((own, att_streams))
    exp_streams = ring_gather(exp_part, own, group_index)
    gu_nb = gu_size // row_width
    gate_up = unpack(exp_streams, exp_part.gather_place[:gu_nb]).reshape(local_experts, D, 2 * FF)
    down = unpack(exp_streams, exp_part.gather_place[gu_nb:]).reshape(local_experts, FF, D)
    q_nb = (query_end - col_size) // row_width
    kv_nb = (keyval_end - col_size) // row_width
    o_nb = (out_end - col_size) // row_width
    att_place = att_part.gather_place
    w_query = unpack(att_streams, att_place[:q_nb])
    w_keyval = unpack(att_streams, att_place[q_nb:kv_nb])
    w_out = unpack(att_streams, att_place[kv_nb:o_nb])
    gains = unpack(att_streams, att_place[o_nb:])[: 4].astype(jnp.float32)
    group_ids = token_ids.reshape(shards * length)
    local_ids = group_ids - shard_index * vocab_rows
    inside = (local_ids >= 0) & (local_ids < vocab_rows)
    safe_ids = jnp.clip(local_ids, 0, vocab_rows - 1)
    found = jnp.where(inside[:, None], table[safe_ids], jnp.zeros((), jnp.bfloat16))
    x_embed = embed_scale * lax.psum_scatter(found, "ep", scatter_dimension=0, tiled=True).astype(
        jnp.float32
    )
    cosine, sine_table = rope_tables(length)
    score_scale = HD ** (-0.5)
    causal = jnp.arange(length)[:, None] >= jnp.arange(length)[None, :]
    normed = rms_norm(x_embed, gains[0]).astype(jnp.bfloat16)
    query = jnp.dot(normed, w_query, preferred_element_type=jnp.float32).reshape(length, HEADS, HD)
    keyval = jnp.dot(normed, w_keyval, preferred_element_type=jnp.float32).reshape(
        length, 2, KV, HD
    )
    query_low = (
        rotate(query, cosine, sine_table).astype(jnp.bfloat16).reshape(length, KV, groups_per, HD)
    )
    keys_low = rotate(keyval[:, 0], cosine, sine_table).astype(jnp.bfloat16)
    values_low = keyval[:, 1].astype(jnp.bfloat16)

    def score_block():
        scores = (
            jnp.einsum("tkgd,skd->kgts", query_low, keys_low, preferred_element_type=jnp.float32)
            * score_scale
        )
        return jnp.where(causal, scores, MASK_FILL)

    scores = score_block()
    peak_score = jnp.max(scores, axis=-1, keepdims=True)
    expo = jnp.exp(scores - peak_score)
    denom = jnp.sum(expo, axis=-1, keepdims=True)
    log_denom = peak_score + jnp.log(denom)
    probs_low = (expo / denom).astype(jnp.bfloat16)
    attended = jnp.einsum(
        "kgts,skd->tkgd", probs_low, values_low, preferred_element_type=jnp.float32
    )
    attended = attended.reshape(length, HEADS * HD).astype(jnp.bfloat16)
    x_attn = x_embed + jnp.dot(attended, w_out, preferred_element_type=jnp.float32)
    pair_slot, slot_pair = slot_tables(expert_routes.reshape(length, TOP))
    mixing = route_weights.reshape(length, TOP)
    mixed = rms_norm(x_attn, gains[1]).astype(jnp.bfloat16)
    pad_rows = jnp.concatenate([mixed, jnp.zeros((1, D), jnp.bfloat16)], axis=0)
    send_token = jnp.where(slot_pair < length * TOP, slot_pair // TOP, length)
    outgoing = pad_rows[send_token].reshape(shards, local_experts * CAP_EXP, D)
    arrived = lax.all_to_all(outgoing, "ep", split_axis=0, concat_axis=0, tiled=True).reshape(
        shards, local_experts, CAP_EXP, D
    )
    gate_val = jnp.einsum("sjcd,jdf->sjcf", arrived, gate_up, preferred_element_type=jnp.float32)
    gate_part = gate_val[..., :FF]
    up_part = gate_val[..., FF:]
    sigma = jax.nn.sigmoid(gate_part)
    hidden = (gate_part * sigma * up_part).astype(jnp.bfloat16)
    produced = jnp.einsum(
        "sjcf,jfd->sjcd", hidden, down, preferred_element_type=jnp.float32
    ).astype(jnp.bfloat16)
    returned = lax.all_to_all(
        produced.reshape(shards, local_experts * CAP_EXP, D),
        "ep",
        split_axis=0,
        concat_axis=0,
        tiled=True,
    )
    chosen = (
        returned.reshape(EXPERTS * CAP_EXP, D)[pair_slot]
        .reshape(length, TOP, D)
        .astype(jnp.float32)
    )
    x_final = x_attn + jnp.sum(mixing[:, :, None] * chosen, axis=1)
    places = action_positions.reshape(act_count)
    final = rms_norm(x_final, gains[2])
    picked = final[places]
    value_pred = jnp.dot(picked, gains[3], precision=lax.Precision.HIGHEST)
    group_rows = lax.all_gather(picked.astype(jnp.bfloat16), "ep", axis=0, tiled=True)
    logits = jnp.einsum("ad,vd->av", group_rows, table, preferred_element_type=jnp.float32)
    targets = action_tokens.reshape(shards * act_count) - shard_index * vocab_rows
    target_mask = jnp.arange(vocab_rows, dtype=jnp.int32)[None, :] == targets[:, None]
    target_logit = jnp.sum(jnp.where(target_mask, logits, 0.0), axis=1)
    local_peak = jnp.max(logits, axis=1)
    local_mass = jnp.sum(jnp.exp(logits - local_peak[:, None]), axis=1)
    all_peak, all_mass, all_target = combined_all(
        (local_peak, local_mass, target_logit), "ep", combine_stats
    )
    log_norm = all_peak + jnp.log(all_mass)
    logp = all_target - log_norm
    group_adv = advantages.reshape(shards * act_count)
    own_logp = lax.dynamic_slice_in_dim(logp, shard_index * act_count, act_count)
    own_adv = lax.dynamic_slice_in_dim(group_adv, shard_index * act_count, act_count)
    own_targets = value_targets.reshape(act_count)
    local_loss = jnp.sum(-own_adv * own_logp + VALUE_COEF * (value_pred - own_targets) ** 2)
    soft = jnp.exp(logits - log_norm[:, None])
    d_logits = ((group_adv / npos)[:, None] * (soft - target_mask.astype(jnp.float32))).astype(
        jnp.bfloat16
    )
    grad_table = jnp.einsum("av,ad->vd", d_logits, group_rows, preferred_element_type=jnp.float32)
    head_part = jnp.einsum("av,vd->ad", d_logits, table, preferred_element_type=jnp.float32)
    grad_picked = lax.psum_scatter(head_part, "ep", scatter_dimension=0, tiled=True)
    grad_value = 2.0 * VALUE_COEF * (value_pred - own_targets) / npos
    grad_picked = grad_picked + grad_value[:, None] * gains[3][None, :]
    grad_vhead = jnp.dot(grad_value, picked, precision=lax.Precision.HIGHEST)
    grad_final = jnp.zeros((length, D), jnp.float32).at[places].add(grad_picked)
    _, final_back = jax.vjp(rms_norm, x_final, gains[2])
    grad_x_final, grad_gain_two = final_back(grad_final)
    grad_pairs = (
        (mixing[:, :, None] * grad_x_final[:, None, :])
        .reshape(length * TOP, D)
        .astype(jnp.bfloat16)
    )
    grad_pad = jnp.concatenate([grad_pairs, jnp.zeros((1, D), jnp.bfloat16)], axis=0)
    grad_outgoing = grad_pad[slot_pair].reshape(shards, local_experts * CAP_EXP, D)
    grad_arrived = lax.all_to_all(
        grad_outgoing, "ep", split_axis=0, concat_axis=0, tiled=True
    ).reshape(shards, local_experts, CAP_EXP, D)
    grad_down = jnp.einsum(
        "sjcf,sjcd->jfd", hidden, grad_arrived, preferred_element_type=jnp.float32
    )
    grad_hidden = jnp.einsum(
        "sjcd,jfd->sjcf", grad_arrived, down, preferred_element_type=jnp.float32
    )
    grad_gate = grad_hidden * up_part * sigma * (1.0 + gate_part * (1.0 - sigma))
    grad_up = grad_hidden * gate_part * sigma
    grad_gate_val = jnp.concatenate([grad_gate, grad_up], axis=-1).astype(jnp.bfloat16)
    grad_gate_up = jnp.einsum(
        "sjcd,sjcf->jdf", arrived, grad_gate_val, preferred_element_type=jnp.float32
    )
    grad_inputs = jnp.einsum(
        "sjcf,jdf->sjcd", grad_gate_val, gate_up, preferred_element_type=jnp.float32
    ).astype(jnp.bfloat16)
    grad_back = lax.all_to_all(
        grad_inputs.reshape(shards, local_experts * CAP_EXP, D),
        "ep",
        split_axis=0,
        concat_axis=0,
        tiled=True,
    )
    grad_mixed = jnp.sum(
        grad_back.reshape(EXPERTS * CAP_EXP, D)[pair_slot]
        .reshape(length, TOP, D)
        .astype(jnp.float32),
        axis=1,
    )
    _, mixed_back = jax.vjp(rms_norm, x_attn, gains[1])
    grad_norm_in, grad_gain_one = mixed_back(grad_mixed)
    grad_x_attn = grad_x_final + grad_norm_in
    grad_attn_low = grad_x_attn.astype(jnp.bfloat16)
    grad_w_out = jnp.einsum(
        "ti,td->id", attended, grad_attn_low, preferred_element_type=jnp.float32
    )
    grad_attended = jnp.einsum(
        "td,id->ti", grad_attn_low, w_out, preferred_element_type=jnp.float32
    )
    grad_attended = grad_attended.astype(jnp.bfloat16).reshape(length, KV, groups_per, HD)
    probs = jnp.exp(score_block() - log_denom)
    probs_again = probs.astype(jnp.bfloat16)
    grad_values = jnp.einsum(
        "kgts,tkgd->skd", probs_again, grad_attended, preferred_element_type=jnp.float32
    )
    grad_probs = jnp.einsum(
        "tkgd,skd->kgts", grad_attended, values_low, preferred_element_type=jnp.float32
    )
    row_delta = jnp.sum(grad_probs * probs, axis=-1, keepdims=True)
    grad_scores = (probs * (grad_probs - row_delta)).astype(jnp.bfloat16)
    grad_query = (
        jnp.einsum("kgts,skd->tkgd", grad_scores, keys_low, preferred_element_type=jnp.float32)
        * score_scale
    )
    grad_keys = (
        jnp.einsum("kgts,tkgd->skd", grad_scores, query_low, preferred_element_type=jnp.float32)
        * score_scale
    )
    grad_query = (
        rotate_back(grad_query.reshape(length, HEADS, HD), cosine, sine_table)
        .reshape(length, HEADS * HD)
        .astype(jnp.bfloat16)
    )
    grad_keys = rotate_back(grad_keys, cosine, sine_table)
    grad_keyval = (
        jnp.stack([grad_keys, grad_values], axis=1)
        .reshape(length, 2 * KV * HD)
        .astype(jnp.bfloat16)
    )
    grad_w_query = jnp.einsum("td,ti->di", normed, grad_query, preferred_element_type=jnp.float32)
    grad_w_keyval = jnp.einsum("td,ti->di", normed, grad_keyval, preferred_element_type=jnp.float32)
    grad_normed = jnp.einsum(
        "ti,di->td", grad_query, w_query, preferred_element_type=jnp.float32
    ) + jnp.einsum("ti,di->td", grad_keyval, w_keyval, preferred_element_type=jnp.float32)
    _, embed_back = jax.vjp(rms_norm, x_embed, gains[0])
    grad_norm_embed, grad_gain_zero = embed_back(grad_normed)
    grad_rows = (embed_scale * (grad_x_attn + grad_norm_embed)).astype(jnp.bfloat16)
    all_rows = lax.all_gather(grad_rows, "ep", axis=0, tiled=True)
    grad_table = grad_table + jax.ops.segment_sum(
        jnp.where(inside[:, None], all_rows.astype(jnp.float32), 0.0),
        safe_ids,
        num_segments=vocab_rows,
    )
    grad_gains = jnp.stack([grad_gain_zero, grad_gain_one, grad_gain_two, grad_vhead])
    att_grads = lax.psum((grad_w_query, grad_w_keyval, grad_w_out, grad_gains), "ep")
    att_rows = jnp.concatenate([piece.reshape(-1, D) for piece in att_grads], axis=0)
    exp_sums = pack(grad_gate_up.reshape(-1, D), exp_part.scatter_place[:gu_nb], exp_part.size)
    exp_sums = pack(
        grad_down.reshape(-1, D), exp_part.scatter_place[gu_nb:], exp_part.size, exp_sums
    )
    exp_sums = ring_scatter(exp_part, exp_sums)
    tab_sums = ring_scatter(tab_part, pack(grad_table, tab_part.scatter_place, tab_part.size))
    att_sums = ring_scatter(att_part, pack(att_rows, att_part.scatter_place, att_part.size))
    row = jnp.arange(capacity, dtype=jnp.int32)
    valid = pick(counts_before, group_index)
    filled = row < valid
    own_col = pick(att_part.base, group_index)
    pieces = []
    for part, sums in ((exp_part, exp_sums), (tab_part, tab_sums), (att_part, att_sums)):
        pieces.append((own_index(part, group_index, row, 0), sums))
    place = jnp.zeros((capacity,), jnp.int32)
    offset = 0
    ups = jnp.concatenate([s[0] for _, s in pieces], axis=0)
    downs = jnp.concatenate([s[1] for _, s in pieces], axis=0)
    whole = ups.shape[0]
    for part, ((inside_part, at), sums) in zip((exp_part, tab_part, att_part), pieces):
        at = jnp.where(at < part.size, at + offset, at - part.size + offset + whole)
        place = jnp.where(inside_part, at, place)
        offset += part.size
    owned = take_blocks((ups, downs), place)
    counted = (filled & ((row < own_col) | (shard_index == 0))).reshape(capacity, 1, 1)
    wide_owned = owned.astype(jnp.float32)
    square = jnp.sum(jnp.where(counted, wide_owned * wide_owned, 0.0))
    square_all, loss_all = lax.psum((square, local_loss), ("grp", "ep"))
    grad_norm = jnp.sqrt(square_all)
    factor = jnp.minimum(1.0, CLIP_BASE / math.sqrt(npos) / grad_norm)
    outs = update(
        factor,
        valid,
        owned,
        master_rows,
        first_moment.reshape(capacity, sub, LANES),
        second_moment.reshape(capacity, sub, LANES),
    )
    return (loss_all / npos, grad_norm) + tuple(o.reshape(master_weights.shape) for o in outs)


def solution(mesh):
    placed = (
        P("grp", None, None),
        P("grp", "ep", None, None),
        P("grp", "ep", None, None),
        P("grp", "ep", None),
        P("grp", None, None),
        P("grp", None, None),
        P("grp", "ep", None),
        P(),
        P("grp", "ep", None),
        P("grp", "ep", None),
        P("grp", "ep", None),
    )
    return jax.shard_map(
        on_device,
        mesh=mesh,
        in_specs=placed,
        out_specs=(P(), P(), P("grp", "ep", None), P("grp", "ep", None), P("grp", "ep", None)),
        check_vma=False,
    )
```

```python
import functools
import math

import jax
import jax.numpy as jnp
from jax import lax
from jax.experimental import pallas as pl
from jax.experimental.pallas import tpu as pltpu
from jax.sharding import PartitionSpec as P

D = 1024
HEADS = 16
KV = 8
HD = 64
FF = 512
EXPERTS = 32
TOP = 8
VOCAB = 49216
ADAM_STEP = 10
CAP_EXP = 96


NORM_EPS = 1e-06
VALUE_COEF = 0.5
CLIP_BASE = 24.0
LEARN_RATE = 0.01
BETA_ONE = 0.9
BETA_TWO = 0.95
ADAM_EPS = 1e-08
WEIGHT_DECAY = 0.1
ROPE_BASE = 10000.0
MASK_FILL = -1e30
LANES = 128
CHUNK = 128
BATCH = 64


def rms_norm(values, gain_row):
    return (
        values * lax.rsqrt(jnp.mean(values * values, axis=-1, keepdims=True) + NORM_EPS) * gain_row
    )


def rope_tables(length):
    positions = jnp.arange(length).astype(jnp.float32)
    inverse = ROPE_BASE ** (-2.0 * jnp.arange(HD // 2).astype(jnp.float32) / HD)
    angles = positions[:, None] * inverse[None, :]
    return (jnp.cos(angles)[:, None, :], jnp.sin(angles)[:, None, :])


def rotate(values, cosine, sine_table):
    half_size = values.shape[-1] // 2
    front = values[..., :half_size]
    behind = values[..., half_size:]
    return jnp.concatenate(
        [front * cosine - behind * sine_table, behind * cosine + front * sine_table], axis=-1
    )


def rotate_back(values, cosine, sine_table):
    half_size = values.shape[-1] // 2
    front = values[..., :half_size]
    behind = values[..., half_size:]
    return jnp.concatenate(
        [front * cosine + behind * sine_table, behind * cosine - front * sine_table], axis=-1
    )


def ring_order(count):
    side = math.isqrt(count)
    if side * side != count or side % 2:
        return list(range(count))
    path = []
    for y in range(side):
        row = range(1, side) if y % 2 == 0 else range(side - 1, 0, -1)
        path += [y * side + x for x in row]
    path += [y * side for y in range(side - 1, -1, -1)]
    return path


def cast_kernel(src_ref, out_ref):
    out_ref[...] = src_ref[...].astype(jnp.bfloat16)


def cast_rows(rows, extra):
    count, sub, _ = rows.shape
    return pl.pallas_call(
        cast_kernel,
        out_shape=jax.ShapeDtypeStruct((count + extra, sub, LANES), jnp.bfloat16),
        grid=(pl.cdiv(count, BATCH),),
        in_specs=[pl.BlockSpec((BATCH, sub, LANES), lambda i: (i, 0, 0))],
        out_specs=pl.BlockSpec((BATCH, sub, LANES), lambda i: (i, 0, 0)),
        name="cast_rows",
    )(rows)


def fetch_blocks(idx_ref, first_ref, second_ref, buf, sem, step, slot):
    limit = first_ref.shape[0]

    def body(k, carry):
        b = idx_ref[step * BATCH + k]

        @pl.when(b < limit)
        def _():
            pltpu.make_async_copy(first_ref.at[b], buf.at[slot, k], sem.at[slot]).start()

        @pl.when(b >= limit)
        def _():
            pltpu.make_async_copy(second_ref.at[b - limit], buf.at[slot, k], sem.at[slot]).start()

        return carry

    lax.fori_loop(0, BATCH, body, 0, unroll=8)


def unpack_kernel(idx_ref, first_ref, second_ref, out_ref, buf, wide, sem):
    i = pl.program_id(0)
    slot = lax.rem(i, 2)

    @pl.when(i == 0)
    def _():
        fetch_blocks(idx_ref, first_ref, second_ref, buf, sem, 0, 0)

    @pl.when(i + 1 < pl.num_programs(0))
    def _():
        fetch_blocks(idx_ref, first_ref, second_ref, buf, sem, i + 1, 1 - slot)

    pltpu.make_async_copy(first_ref.at[pl.ds(0, BATCH)], buf.at[slot], sem.at[slot]).wait()
    sub = buf.shape[2]
    per = D // LANES
    wide[...] = buf[slot].astype(jnp.float32).reshape(BATCH * sub, LANES)
    for j in range(per):
        out_ref[:, LANES * j : LANES * (j + 1)] = wide[
            pl.ds(j, BATCH * sub // per, stride=per), :
        ].astype(jnp.bfloat16)


def pad_index(index):
    count = index.shape[0]
    return jnp.pad(index, (0, pl.cdiv(count, BATCH) * BATCH - count)).astype(jnp.int32)


def unpack(streams, index):
    first, second = streams
    count = index.shape[0]
    sub = first.shape[1]
    rows = sub * LANES // D
    return pl.pallas_call(
        unpack_kernel,
        out_shape=jax.ShapeDtypeStruct((count * rows, D), jnp.bfloat16),
        grid_spec=pltpu.PrefetchScalarGridSpec(
            num_scalar_prefetch=1,
            grid=(pl.cdiv(count, BATCH),),
            in_specs=[pl.BlockSpec(memory_space=pl.ANY), pl.BlockSpec(memory_space=pl.ANY)],
            out_specs=pl.BlockSpec((BATCH * rows, D), lambda i, idx: (i, 0)),
            scratch_shapes=[
                pltpu.VMEM((2, BATCH, sub, LANES), jnp.bfloat16),
                pltpu.VMEM((BATCH * sub, LANES), jnp.float32),
                pltpu.SemaphoreType.DMA((2,)),
            ],
        ),
        cost_estimate=pl.CostEstimate(
            flops=0, bytes_accessed=4 * count * sub * LANES, transcendentals=0
        ),
        name="unpack",
    )(pad_index(index), first, second)


def own_kernel(limits, idx_ref, *refs):
    sources = refs[: len(limits)]
    out_ref, buf, sem = refs[len(limits) :]
    i = pl.program_id(0)
    slot = lax.rem(i, 2)

    def fetch(step, which):
        def body(k, carry):
            b = idx_ref[step * BATCH + k]
            start = 0
            for source, limit in zip(sources, limits):

                @pl.when((b >= start) & (b < start + limit))
                def _(source=source, start=start):
                    pltpu.make_async_copy(
                        source.at[b - start], buf.at[which, k], sem.at[which]
                    ).start()

                start += limit
            return carry

        lax.fori_loop(0, BATCH, body, 0, unroll=8)

    @pl.when(i == 0)
    def _():
        fetch(0, 0)

    @pl.when(i + 1 < pl.num_programs(0))
    def _():
        fetch(i + 1, 1 - slot)

    pltpu.make_async_copy(sources[0].at[pl.ds(0, BATCH)], buf.at[slot], sem.at[slot]).wait()
    out_ref[...] = buf[slot]


def take_blocks(streams, index):
    count = index.shape[0]
    sub = streams[0].shape[1]
    return pl.pallas_call(
        functools.partial(own_kernel, tuple(s.shape[0] for s in streams)),
        out_shape=jax.ShapeDtypeStruct((count, sub, LANES), jnp.bfloat16),
        grid_spec=pltpu.PrefetchScalarGridSpec(
            num_scalar_prefetch=1,
            grid=(pl.cdiv(count, BATCH),),
            in_specs=[pl.BlockSpec(memory_space=pl.ANY)] * len(streams),
            out_specs=pl.BlockSpec((BATCH, sub, LANES), lambda i, idx: (i, 0, 0)),
            scratch_shapes=[
                pltpu.VMEM((2, BATCH, sub, LANES), jnp.bfloat16),
                pltpu.SemaphoreType.DMA((2,)),
            ],
        ),
        name="take_blocks",
    )(pad_index(index), *streams)


def pack_kernel(count, keep, idx_ref, src_ref, *refs):
    first_ref, second_ref, wide, buf, sem = refs[2:] if keep else refs
    i = pl.program_id(0)
    steps = pl.num_programs(0)
    slot = lax.rem(i, 2)
    limit = first_ref.shape[0]
    sub = buf.shape[2]
    per = D // LANES
    last = count - (pl.cdiv(count, BATCH) - 1) * BATCH

    def drain(which, blocks):
        pltpu.make_async_copy(
            buf.at[which, pl.ds(0, blocks)], first_ref.at[pl.ds(0, blocks)], sem.at[which]
        ).wait()

    @pl.when(i >= 2)
    def _():
        drain(slot, BATCH)

    for j in range(per):
        wide[pl.ds(j, BATCH * sub // per, stride=per), :] = src_ref[
            :, LANES * j : LANES * (j + 1)
        ].astype(jnp.float32)
    buf[slot] = wide[...].reshape(BATCH, sub, LANES).astype(jnp.bfloat16)

    def body(k, carry):
        b = idx_ref[i * BATCH + k]

        @pl.when(b < limit)
        def _():
            pltpu.make_async_copy(buf.at[slot, k], first_ref.at[b], sem.at[slot]).start()

        @pl.when(b >= limit)
        def _():
            pltpu.make_async_copy(buf.at[slot, k], second_ref.at[b - limit], sem.at[slot]).start()

        return carry

    @pl.when(i < steps - 1)
    def _():
        lax.fori_loop(0, BATCH, body, 0, unroll=8)

    @pl.when(i == steps - 1)
    def _():
        lax.fori_loop(0, last, body, 0)
        drain(slot, last)

        @pl.when(i >= 1)
        def _():
            drain(1 - slot, BATCH)


def pack(grad, index, size, streams=None):
    count = index.shape[0]
    rows = grad.shape[0] // count
    sub = rows * D // LANES
    keep = streams is not None
    shape = jax.ShapeDtypeStruct((size, sub, LANES), jnp.bfloat16)
    anywhere = pl.BlockSpec(memory_space=pl.ANY)
    return pl.pallas_call(
        functools.partial(pack_kernel, count, keep),
        out_shape=(shape, shape),
        grid_spec=pltpu.PrefetchScalarGridSpec(
            num_scalar_prefetch=1,
            grid=(pl.cdiv(count, BATCH),),
            in_specs=[pl.BlockSpec((BATCH * rows, D), lambda i, idx: (i, 0))]
            + ([anywhere, anywhere] if keep else []),
            out_specs=(anywhere, anywhere),
            scratch_shapes=[
                pltpu.VMEM((BATCH * sub, LANES), jnp.float32),
                pltpu.VMEM((2, BATCH, sub, LANES), jnp.bfloat16),
                pltpu.SemaphoreType.DMA((2,)),
            ],
        ),
        input_output_aliases={2: 0, 3: 1} if keep else {},
        cost_estimate=pl.CostEstimate(
            flops=0, bytes_accessed=6 * count * sub * LANES, transcendentals=0
        ),
        name="pack",
    )(pad_index(index), grad, *(streams if keep else ()))


def update_kernel(scal_ref, count_ref, grad_ref, m_ref, f_ref, s_ref, om_ref, of_ref, os_ref):
    i = pl.program_id(0)
    rows = grad_ref.shape[0]
    row = i * rows + lax.broadcasted_iota(jnp.int32, grad_ref.shape, 0)
    keep = row < count_ref[0]
    clipped = scal_ref[0] * grad_ref[...].astype(jnp.float32)
    master = m_ref[...]
    new_first = BETA_ONE * f_ref[...] + (1.0 - BETA_ONE) * clipped
    new_second = BETA_TWO * s_ref[...] + (1.0 - BETA_TWO) * clipped * clipped
    step_size = (
        new_first
        / (1.0 - BETA_ONE**ADAM_STEP)
        / (jnp.sqrt(new_second / (1.0 - BETA_TWO**ADAM_STEP)) + ADAM_EPS)
    )
    new_master = master - LEARN_RATE * (step_size + WEIGHT_DECAY * master)
    om_ref[...] = jnp.where(keep, new_master, 0.0)
    of_ref[...] = jnp.where(keep, new_first, 0.0)
    os_ref[...] = jnp.where(keep, new_second, 0.0)


def update(factor, valid, grad, master, first, second):
    count, sub, _ = grad.shape
    tile = next(t for t in range(64, 0, -1) if count % t == 0)
    spec = pl.BlockSpec((tile, sub, LANES), lambda i, a, b: (i, 0, 0))
    shape = jax.ShapeDtypeStruct(grad.shape, jnp.float32)
    return pl.pallas_call(
        update_kernel,
        out_shape=(shape, shape, shape),
        grid_spec=pltpu.PrefetchScalarGridSpec(
            num_scalar_prefetch=2,
            grid=(count // tile,),
            in_specs=[spec] * 4,
            out_specs=(spec, spec, spec),
        ),
        name="update",
    )(factor.reshape(1), valid.reshape(1), grad, master, first, second)


class Part:
    def __init__(self, lo, hi, member, before, counts_before, ring_pos, my_pos):
        groups = member.shape[1]
        self.lo, self.count, self.groups = lo, hi - lo, groups
        self.size = (hi - lo) // 2 + groups + (groups + 1) * CHUNK
        inside = member[lo:hi]
        self.held = jnp.sum(inside, axis=0)
        self.base = counts_before
        rank = jnp.sum((before[lo:hi] - counts_before[None, :]) * inside, axis=1)
        half = (self.held + 1) // 2
        halves = (half, self.held - half)
        self.half = half
        self.steps = []
        self.gather_seg, self.scatter_seg, self.lag, self.scatter_lag = [], [], [], []
        padded_sum = []
        steps = jnp.zeros((), jnp.int32)
        slots = jnp.arange(groups, dtype=jnp.int32)
        for way in (0, 1):
            wide = jnp.maximum(halves[way], CHUNK)
            at_ring = jnp.sum(jnp.where(ring_pos[None, :] == slots[:, None], wide[None, :], 0), axis=1)
            steps = jnp.maximum(steps, jnp.max(jnp.sum(at_ring) - at_ring))
            turn = 1 if way == 0 else -1

            def starts(origin):
                gap = ((origin - slots) * turn) % groups
                earlier = gap[None, :] < gap[:, None]
                return jnp.sum(jnp.where(earlier, at_ring[None, :], 0), axis=1)

            def by_group(ring_values):
                return jnp.sum(
                    jnp.where(ring_pos[:, None] == slots[None, :], ring_values[None, :], 0), axis=1
                )

            here = jnp.sum(jnp.where(slots == my_pos, at_ring, 0))
            prev = jnp.sum(jnp.where(slots == (my_pos - turn) % groups, at_ring, 0))
            self.lag.append(here)
            self.scatter_lag.append(prev)
            self.gather_seg.append(by_group(starts(my_pos)))
            self.scatter_seg.append(by_group(starts((my_pos - turn) % groups)))
        self.dyn_steps = (steps + CHUNK - 1) // CHUNK
        self.fixed_steps = int(0.45 * (hi - lo)) // CHUNK

        def place(seg):
            up = jnp.sum((seg[0])[None, :] * inside, axis=1) + rank
            down = jnp.sum((seg[1] - half)[None, :] * inside, axis=1) + rank + self.size
            return jnp.where(rank < jnp.sum(half[None, :] * inside, axis=1), up, down)

        self.gather_place = place(self.gather_seg)
        self.scatter_place = place(self.scatter_seg)


def ring_links(count):
    order = ring_order(count)
    up = [(order[k], order[(k + 1) % count]) for k in range(count)]
    return up, [(b, a) for a, b in up]


def pick(vector, index):
    return jnp.sum(jnp.where(jnp.arange(vector.shape[0]) == index, vector, 0))


def run_ring(part, streams, step):
    for s in range(part.fixed_steps):
        streams = [step(s, way, streams[way]) for way in (0, 1)]

    def body(s, carry):
        return tuple(step(s, way, carry[way]) for way in (0, 1))

    return lax.fori_loop(part.fixed_steps, part.dyn_steps, body, tuple(streams))


def ring_gather(part, own, group_index):
    links = ring_links(part.groups)
    base = pick(part.base, group_index)
    half = pick(part.half, group_index)
    streams = [
        lax.dynamic_slice_in_dim(own, start, part.size) for start in (base, base + half)
    ]

    def step(s, way, stream):
        sent = lax.dynamic_slice_in_dim(stream, s * CHUNK, CHUNK)
        got = lax.ppermute(sent, "grp", links[way])
        at = jnp.minimum(part.lag[way] + s * CHUNK, part.size - CHUNK)
        return lax.dynamic_update_slice_in_dim(stream, got, at, 0)

    return run_ring(part, streams, step)


def ring_scatter(part, streams):
    links = ring_links(part.groups)

    def step(s, way, stream):
        sent = lax.dynamic_slice_in_dim(stream, s * CHUNK, CHUNK)
        got = lax.ppermute(sent, "grp", links[way])
        at = jnp.minimum(part.scatter_lag[way] + s * CHUNK, part.size - CHUNK)
        old = lax.dynamic_slice_in_dim(stream, at, CHUNK)
        total = (old.astype(jnp.float32) + got.astype(jnp.float32)).astype(jnp.bfloat16)
        return lax.dynamic_update_slice_in_dim(stream, total, at, 0)

    return run_ring(part, streams, step)


def own_index(part, group_index, row, offset):
    k = row - pick(part.base, group_index)
    half = pick(part.half, group_index)
    up = pick(part.scatter_seg[0], group_index) + k
    down = pick(part.scatter_seg[1], group_index) + k - half + part.size
    inside = (k >= 0) & (k < pick(part.held, group_index))
    return inside, jnp.where(k < half, up, down) + offset


def sum_everywhere(values):
    values = jnp.zeros((8, LANES), jnp.float32).at[0, : values.shape[0]].set(values)
    for axis in ("ep", "grp"):
        size = lax.axis_size(axis)
        step = 1
        while step < size:
            pairs = [(k, k ^ step) for k in range(size)]
            values = values + lax.ppermute(values, axis, pairs)
            step *= 2
    return values[0, 0], values[0, 1]


def on_device(
    token_ids,
    expert_routes,
    route_weights,
    action_positions,
    action_tokens,
    advantages,
    value_targets,
    owners,
    master_weights,
    first_moment,
    second_moment,
):
    groups = lax.axis_size("grp")
    shards = lax.axis_size("ep")
    group_index = lax.axis_index("grp")
    shard_index = lax.axis_index("ep")
    capacity = master_weights.shape[0]
    row_width = master_weights.shape[2]
    blocks = owners.shape[0]
    length = token_ids.shape[2]
    act_count = action_positions.shape[2]
    local_experts = EXPERTS // shards
    vocab_rows = VOCAB // shards
    npos = groups * shards * act_count
    groups_per = HEADS // KV
    embed_scale = math.sqrt(D) / 2.0
    gu_size = local_experts * D * 2 * FF
    dn_size = local_experts * FF * D
    col_size = gu_size + dn_size + vocab_rows * D
    query_end = col_size + D * HEADS * HD
    keyval_end = query_end + D * 2 * KV * HD
    out_end = keyval_end + HEADS * HD * D
    sub = row_width // LANES
    order = ring_order(groups)
    ring_pos = jnp.array([order.index(g) for g in range(groups)], jnp.int32)
    my_pos = pick(ring_pos, group_index)
    member = (owners[:, None] == jnp.arange(groups, dtype=jnp.int32)[None, :]).astype(jnp.int32)
    before = jnp.cumsum(member, axis=0) - member
    marks = [0, (gu_size + dn_size) // row_width, col_size // row_width, blocks]
    parts = []
    counts_before = jnp.zeros((groups,), jnp.int32)
    for lo, hi in zip(marks[:-1], marks[1:]):
        parts.append(Part(lo, hi, member, before, counts_before, ring_pos, my_pos))
        counts_before = counts_before + parts[-1].held
    exp_part, tab_part, att_part = parts
    master_rows = master_weights.reshape(capacity, sub, LANES)
    own = cast_rows(master_rows, max(part.size for part in parts))
    tab_streams = ring_gather(tab_part, own, group_index)
    own, tab_streams = lax.optimization_barrier((own, tab_streams))
    table = unpack(tab_streams, tab_part.gather_place)
    att_streams = ring_gather(att_part, own, group_index)
    own, att_streams = lax.optimization_barrier((own, att_streams))
    exp_streams = ring_gather(exp_part, own, group_index)
    gu_nb = gu_size // row_width
    gate_up = unpack(exp_streams, exp_part.gather_place[:gu_nb]).reshape(local_experts, D, 2 * FF)
    down = unpack(exp_streams, exp_part.gather_place[gu_nb:]).reshape(local_experts, FF, D)
    q_nb = (query_end - col_size) // row_width
    kv_nb = (keyval_end - col_size) // row_width
    o_nb = (out_end - col_size) // row_width
    att_place = att_part.gather_place
    w_query = unpack(att_streams, att_place[:q_nb])
    w_keyval = unpack(att_streams, att_place[q_nb:kv_nb])
    w_out = unpack(att_streams, att_place[kv_nb:o_nb])
    gains = unpack(att_streams, att_place[o_nb:])[: 4].astype(jnp.float32)
    group_ids = token_ids.reshape(shards * length)
    local_ids = group_ids - shard_index * vocab_rows
    inside = (local_ids >= 0) & (local_ids < vocab_rows)
    safe_ids = jnp.clip(local_ids, 0, vocab_rows - 1)
    found = jnp.where(inside[:, None], table[safe_ids], jnp.zeros((), jnp.bfloat16))
    x_embed = embed_scale * lax.psum_scatter(found, "ep", scatter_dimension=0, tiled=True).astype(
        jnp.float32
    )
    places = action_positions.reshape(act_count)
    cosine, sine_table = rope_tables(length)
    score_scale = HD ** (-0.5)
    rows = length
    slots = CAP_EXP
    causal = jnp.arange(length)[:, None] >= jnp.arange(length)[None, :]
    sum_type = jnp.bfloat16

    def take(values):
        return values

    def put(values):
        return values

    cosine_q, sine_q = take(cosine), take(sine_table)
    routing = jnp.concatenate(
        [
            take(expert_routes.reshape(length, TOP)).astype(jnp.float32),
            take(route_weights.reshape(length, TOP)),
        ],
        axis=1,
    )
    routing = lax.all_gather(routing, "ep", axis=0)
    local_ids_exp = shard_index * local_experts + jnp.arange(local_experts, dtype=jnp.int32)
    named = routing[:, :, None, :TOP] == local_ids_exp[None, None, :, None].astype(jnp.float32)
    routed = jnp.sum(named.astype(jnp.float32), axis=3)
    pair_weight = jnp.sum(jnp.where(named, routing[:, :, None, TOP:], 0.0), axis=3)
    earlier_row = (jnp.arange(rows)[:, None] < jnp.arange(rows)[None, :]).astype(jnp.bfloat16)
    slot_of = jnp.einsum(
        "pt,spj->sjt",
        earlier_row,
        routed.astype(jnp.bfloat16),
        preferred_element_type=jnp.float32,
    )
    slot_of = jnp.where(jnp.swapaxes(routed, 1, 2) > 0.0, slot_of, -1.0)
    held = slot_of[:, :, None, :] == jnp.arange(slots, dtype=jnp.float32)[None, None, :, None]
    dealt = held.astype(jnp.bfloat16)
    slot_weight = jnp.sum(
        jnp.where(held, jnp.swapaxes(pair_weight, 1, 2)[:, :, None, :], 0.0), axis=3
    )[..., None]

    def to_experts(values):
        return jnp.einsum("sjcp,spd->sjcd", dealt, values, preferred_element_type=jnp.float32)

    def from_experts(values):
        partial = jnp.einsum(
            "sjcp,sjcd->spd", dealt, values, preferred_element_type=jnp.float32
        ).astype(sum_type)
        return lax.psum_scatter(
            partial.reshape(shards * rows, D), "ep", scatter_dimension=0, tiled=True
        ).astype(jnp.float32)

    normed = rms_norm(x_embed, gains[0]).astype(jnp.bfloat16)
    normed_q = take(normed)
    query = jnp.dot(normed_q, w_query, preferred_element_type=jnp.float32).reshape(rows, HEADS, HD)
    keyval = jnp.dot(normed, w_keyval, preferred_element_type=jnp.float32).reshape(
        length, 2, KV, HD
    )
    query_low = rotate(query, cosine_q, sine_q).astype(jnp.bfloat16)
    query_low = query_low.reshape(rows, KV, groups_per, HD)
    keys_low = rotate(keyval[:, 0], cosine, sine_table).astype(jnp.bfloat16)
    values_low = keyval[:, 1].astype(jnp.bfloat16)

    def score_block():
        scores = (
            jnp.einsum("tkgd,skd->kgts", query_low, keys_low, preferred_element_type=jnp.float32)
            * score_scale
        )
        return jnp.where(causal, scores, MASK_FILL)

    scores = score_block()
    peak_score = jnp.max(scores, axis=-1, keepdims=True)
    expo = jnp.exp(scores - peak_score)
    denom = jnp.sum(expo, axis=-1, keepdims=True)
    log_denom = peak_score + jnp.log(denom)
    probs_low = (expo / denom).astype(jnp.bfloat16)
    attended = jnp.einsum(
        "kgts,skd->tkgd", probs_low, values_low, preferred_element_type=jnp.float32
    )
    attended = attended.reshape(rows, HEADS * HD).astype(jnp.bfloat16)
    x_attn = take(x_embed) + jnp.dot(attended, w_out, preferred_element_type=jnp.float32)
    mixed = rms_norm(x_attn, gains[1]).astype(jnp.bfloat16)
    mixed_all = lax.all_gather(mixed, "ep", axis=0)
    arrived = to_experts(mixed_all).astype(jnp.bfloat16)
    gate_val = jnp.einsum("sjcd,jdf->sjcf", arrived, gate_up, preferred_element_type=jnp.float32)
    gate_part = gate_val[..., :FF]
    up_part = gate_val[..., FF:]
    sigma = jax.nn.sigmoid(gate_part)
    hidden = (gate_part * sigma * up_part).astype(jnp.bfloat16)
    produced = jnp.einsum(
        "sjcf,jfd->sjcd", hidden, down, preferred_element_type=jnp.float32
    ).astype(jnp.bfloat16)
    weighted = (slot_weight * produced.astype(jnp.float32)).astype(jnp.bfloat16)
    x_final = x_attn + from_experts(weighted)
    final = rms_norm(x_final, gains[2])
    picked = final[places]
    value_pred = jnp.dot(picked, gains[3], precision=lax.Precision.HIGHEST)
    group_rows = lax.all_gather(picked.astype(jnp.bfloat16), "ep", axis=0, tiled=True)
    logits = jnp.einsum("ad,vd->av", group_rows, table, preferred_element_type=jnp.float32)
    targets = action_tokens.reshape(shards * act_count) - shard_index * vocab_rows
    target_mask = jnp.arange(vocab_rows, dtype=jnp.int32)[None, :] == targets[:, None]
    target_logit = jnp.sum(jnp.where(target_mask, logits, 0.0), axis=1)
    local_peak = jnp.max(logits, axis=1)
    local_mass = jnp.sum(jnp.exp(logits - local_peak[:, None]), axis=1)
    stats = lax.all_gather(jnp.stack([local_peak, local_mass, target_logit]), "ep", axis=0)
    all_peak = jnp.max(stats[:, 0], axis=0)
    all_mass = jnp.sum(stats[:, 1] * jnp.exp(stats[:, 0] - all_peak[None, :]), axis=0)
    all_target = jnp.sum(stats[:, 2], axis=0)
    log_norm = all_peak + jnp.log(all_mass)
    logp = all_target - log_norm
    group_adv = advantages.reshape(shards * act_count)
    own_logp = lax.dynamic_slice_in_dim(logp, shard_index * act_count, act_count)
    own_adv = lax.dynamic_slice_in_dim(group_adv, shard_index * act_count, act_count)
    own_targets = value_targets.reshape(act_count)
    local_loss = jnp.sum(-own_adv * own_logp + VALUE_COEF * (value_pred - own_targets) ** 2)
    soft = jnp.exp(logits - log_norm[:, None])
    d_logits = ((group_adv / npos)[:, None] * (soft - target_mask.astype(jnp.float32))).astype(
        jnp.bfloat16
    )
    grad_table = jnp.einsum("av,ad->vd", d_logits, group_rows, preferred_element_type=jnp.float32)
    head_part = jnp.einsum("av,vd->ad", d_logits, table, preferred_element_type=jnp.float32)
    grad_picked = lax.psum_scatter(head_part, "ep", scatter_dimension=0, tiled=True)
    grad_value = 2.0 * VALUE_COEF * (value_pred - own_targets) / npos
    grad_picked = grad_picked + grad_value[:, None] * gains[3][None, :]
    grad_vhead = jnp.dot(grad_value, picked, precision=lax.Precision.HIGHEST)
    grad_final = jnp.zeros((length, D), jnp.float32).at[places].add(grad_picked)
    _, final_back = jax.vjp(rms_norm, x_final, gains[2])
    grad_x_final, grad_gain_two = final_back(grad_final)
    grad_final_all = lax.all_gather(grad_x_final.astype(jnp.bfloat16), "ep", axis=0)
    grad_arrived = (slot_weight * to_experts(grad_final_all)).astype(jnp.bfloat16)
    grad_down = jnp.einsum(
        "sjcf,sjcd->jfd", hidden, grad_arrived, preferred_element_type=jnp.float32
    )
    grad_hidden = jnp.einsum(
        "sjcd,jfd->sjcf", grad_arrived, down, preferred_element_type=jnp.float32
    )
    grad_gate = grad_hidden * up_part * sigma * (1.0 + gate_part * (1.0 - sigma))
    grad_up = grad_hidden * gate_part * sigma
    grad_gate_val = jnp.concatenate([grad_gate, grad_up], axis=-1).astype(jnp.bfloat16)
    grad_gate_up = jnp.einsum(
        "sjcd,sjcf->jdf", arrived, grad_gate_val, preferred_element_type=jnp.float32
    )
    grad_inputs = jnp.einsum(
        "sjcf,jdf->sjcd", grad_gate_val, gate_up, preferred_element_type=jnp.float32
    ).astype(jnp.bfloat16)
    grad_mixed = from_experts(grad_inputs)
    _, mixed_back = jax.vjp(rms_norm, x_attn, gains[1])
    grad_norm_in, grad_gain_one = mixed_back(grad_mixed)
    grad_x_attn = grad_x_final + grad_norm_in
    grad_attn_low = grad_x_attn.astype(jnp.bfloat16)
    grad_attended = jnp.einsum(
        "td,id->ti", grad_attn_low, w_out, preferred_element_type=jnp.float32
    )
    grad_attended = grad_attended.astype(jnp.bfloat16).reshape(rows, KV, groups_per, HD)
    probs = jnp.exp(score_block() - log_denom)
    probs_again = probs.astype(jnp.bfloat16)
    grad_values = jnp.einsum(
        "kgts,tkgd->skd", probs_again, grad_attended, preferred_element_type=jnp.float32
    )
    grad_probs = jnp.einsum(
        "tkgd,skd->kgts", grad_attended, values_low, preferred_element_type=jnp.float32
    )
    row_delta = jnp.sum(grad_probs * probs, axis=-1, keepdims=True)
    grad_scores = (probs * (grad_probs - row_delta)).astype(jnp.bfloat16)
    grad_query = (
        jnp.einsum("kgts,skd->tkgd", grad_scores, keys_low, preferred_element_type=jnp.float32)
        * score_scale
    )
    grad_keys = (
        jnp.einsum("kgts,tkgd->skd", grad_scores, query_low, preferred_element_type=jnp.float32)
        * score_scale
    )
    grad_query = (
        rotate_back(grad_query.reshape(rows, HEADS, HD), cosine_q, sine_q)
        .reshape(rows, HEADS * HD)
        .astype(jnp.bfloat16)
    )
    grad_keys = rotate_back(grad_keys, cosine, sine_table)
    grad_keyval = (
        jnp.stack([grad_keys, grad_values], axis=1)
        .reshape(length, 2 * KV * HD)
        .astype(jnp.bfloat16)
    )
    grad_normed = put(
        jnp.einsum("ti,di->td", grad_query, w_query, preferred_element_type=jnp.float32)
    ) + jnp.einsum("ti,di->td", grad_keyval, w_keyval, preferred_element_type=jnp.float32)
    _, embed_back = jax.vjp(rms_norm, x_embed, gains[0])
    grad_norm_embed, grad_gain_zero = embed_back(grad_normed)
    grad_rows = (embed_scale * (put(grad_x_attn) + grad_norm_embed)).astype(jnp.bfloat16)
    grad_gains = jnp.stack([grad_gain_zero, grad_gain_one, grad_gain_two, grad_vhead])
    gains_high = grad_gains.astype(jnp.bfloat16)
    gains_low = (grad_gains - gains_high.astype(jnp.float32)).astype(jnp.bfloat16)
    ahead = lax.all_gather(jnp.concatenate([attended, normed_q, normed], axis=0), "ep", axis=0)
    behind = lax.all_gather(
        jnp.concatenate(
            [grad_attn_low, grad_query, grad_keyval, grad_rows, gains_high, gains_low], axis=0
        ),
        "ep",
        axis=0,
    )

    def outer(ins, outs):
        return jnp.einsum("sti,sto->io", ins, outs, preferred_element_type=jnp.float32)

    grad_w_out = outer(ahead[:, :rows], behind[:, :rows])
    grad_w_query = outer(ahead[:, rows : 2 * rows], behind[:, rows : 2 * rows])
    grad_w_keyval = outer(ahead[:, 2 * rows :], behind[:, 2 * rows : 2 * rows + length])
    all_rows = behind[:, 2 * rows + length : 2 * (rows + length)].reshape(shards * length, D)
    grad_gains = jnp.sum(
        behind[:, 2 * (rows + length) :].astype(jnp.float32).reshape(shards, 2, 4, D),
        axis=(0, 1),
    )
    att_grads = (grad_w_query, grad_w_keyval, grad_w_out, grad_gains)
    grad_table = grad_table + jax.ops.segment_sum(
        jnp.where(inside[:, None], all_rows.astype(jnp.float32), 0.0),
        safe_ids,
        num_segments=vocab_rows,
    )
    att_rows = jnp.concatenate([piece.reshape(-1, D) for piece in att_grads], axis=0)
    exp_sums = pack(grad_gate_up.reshape(-1, D), exp_part.scatter_place[:gu_nb], exp_part.size)
    exp_sums = pack(
        grad_down.reshape(-1, D), exp_part.scatter_place[gu_nb:], exp_part.size, exp_sums
    )
    exp_sums = ring_scatter(exp_part, exp_sums)
    tab_sums = ring_scatter(tab_part, pack(grad_table, tab_part.scatter_place, tab_part.size))
    att_sums = ring_scatter(att_part, pack(att_rows, att_part.scatter_place, att_part.size))
    row = jnp.arange(capacity, dtype=jnp.int32)
    valid = pick(counts_before, group_index)
    filled = row < valid
    own_col = pick(att_part.base, group_index)
    place = jnp.zeros((capacity,), jnp.int32)
    offset = 0
    for part in (exp_part, tab_part, att_part):
        inside_part, at = own_index(part, group_index, row, offset)
        place = jnp.where(inside_part, at, place)
        offset += 2 * part.size
    owned = take_blocks((*exp_sums, *tab_sums, *att_sums), place)
    counted = (filled & ((row < own_col) | (shard_index == 0))).reshape(capacity, 1, 1)
    wide_owned = owned.astype(jnp.float32)
    square = jnp.sum(jnp.where(counted, wide_owned * wide_owned, 0.0))
    square_all, loss_all = sum_everywhere(jnp.stack([square, local_loss]))
    grad_norm = jnp.sqrt(square_all)
    factor = jnp.minimum(1.0, CLIP_BASE / math.sqrt(npos) / grad_norm)
    outs = update(
        factor,
        valid,
        owned,
        master_rows,
        first_moment.reshape(capacity, sub, LANES),
        second_moment.reshape(capacity, sub, LANES),
    )
    return (loss_all / npos, grad_norm) + tuple(o.reshape(master_weights.shape) for o in outs)


def solution(mesh):
    placed = (
        P("grp", None, None),
        P("grp", "ep", None, None),
        P("grp", "ep", None, None),
        P("grp", "ep", None),
        P("grp", None, None),
        P("grp", None, None),
        P("grp", "ep", None),
        P(),
        P("grp", "ep", None),
        P("grp", "ep", None),
        P("grp", "ep", None),
    )
    return jax.shard_map(
        on_device,
        mesh=mesh,
        in_specs=placed,
        out_specs=(P(), P(), P("grp", "ep", None), P("grp", "ep", None), P("grp", "ep", None)),
        check_vma=False,
    )
```

```python
import functools
import math

import jax
import jax.numpy as jnp
from jax import lax
from jax.experimental import pallas as pl
from jax.experimental.pallas import tpu as pltpu
from jax.sharding import PartitionSpec as P

D = 1024
HEADS = 16
KV = 8
HD = 64
FF = 512
EXPERTS = 32
TOP = 8
VOCAB = 49216
ADAM_STEP = 10
CAP_EXP = 96


NORM_EPS = 1e-06
VALUE_COEF = 0.5
CLIP_BASE = 24.0
LEARN_RATE = 0.01
BETA_ONE = 0.9
BETA_TWO = 0.95
ADAM_EPS = 1e-08
WEIGHT_DECAY = 0.1
ROPE_BASE = 10000.0
MASK_FILL = -1e30
LANES = 128
FRESH = 256
BATCH = 64


def rms_norm(values, gain_row):
    return (
        values * lax.rsqrt(jnp.mean(values * values, axis=-1, keepdims=True) + NORM_EPS) * gain_row
    )


def rope_tables(length):
    positions = jnp.arange(length).astype(jnp.float32)
    inverse = ROPE_BASE ** (-2.0 * jnp.arange(HD // 2).astype(jnp.float32) / HD)
    angles = positions[:, None] * inverse[None, :]
    return (jnp.cos(angles)[:, None, :], jnp.sin(angles)[:, None, :])


def rotate(values, cosine, sine_table):
    half_size = values.shape[-1] // 2
    front = values[..., :half_size]
    behind = values[..., half_size:]
    return jnp.concatenate(
        [front * cosine - behind * sine_table, behind * cosine + front * sine_table], axis=-1
    )


def rotate_back(values, cosine, sine_table):
    half_size = values.shape[-1] // 2
    front = values[..., :half_size]
    behind = values[..., half_size:]
    return jnp.concatenate(
        [front * cosine + behind * sine_table, behind * cosine - front * sine_table], axis=-1
    )


def ring_order(count):
    side = math.isqrt(count)
    if side * side != count or side % 2:
        return list(range(count))
    path = []
    for y in range(side):
        row = range(1, side) if y % 2 == 0 else range(side - 1, 0, -1)
        path += [y * side + x for x in row]
    path += [y * side for y in range(side - 1, -1, -1)]
    return path


def cast_kernel(src_ref, out_ref):
    out_ref[...] = src_ref[...].astype(jnp.bfloat16)


def cast_rows(rows, extra):
    count, sub, _ = rows.shape
    return pl.pallas_call(
        cast_kernel,
        out_shape=jax.ShapeDtypeStruct((count + extra, sub, LANES), jnp.bfloat16),
        grid=(pl.cdiv(count, BATCH),),
        in_specs=[pl.BlockSpec((BATCH, sub, LANES), lambda i: (i, 0, 0))],
        out_specs=pl.BlockSpec((BATCH, sub, LANES), lambda i: (i, 0, 0)),
        name="cast_rows",
    )(rows)


def fetch_blocks(idx_ref, first_ref, second_ref, buf, sem, step, slot):
    limit = first_ref.shape[0]

    def body(k, carry):
        b = idx_ref[step * BATCH + k]

        @pl.when(b < limit)
        def _():
            pltpu.make_async_copy(first_ref.at[b], buf.at[slot, k], sem.at[slot]).start()

        @pl.when(b >= limit)
        def _():
            pltpu.make_async_copy(second_ref.at[b - limit], buf.at[slot, k], sem.at[slot]).start()

        return carry

    lax.fori_loop(0, BATCH, body, 0, unroll=8)


def unpack_kernel(idx_ref, first_ref, second_ref, out_ref, buf, wide, sem):
    i = pl.program_id(0)
    slot = lax.rem(i, 2)

    @pl.when(i == 0)
    def _():
        fetch_blocks(idx_ref, first_ref, second_ref, buf, sem, 0, 0)

    @pl.when(i + 1 < pl.num_programs(0))
    def _():
        fetch_blocks(idx_ref, first_ref, second_ref, buf, sem, i + 1, 1 - slot)

    pltpu.make_async_copy(first_ref.at[pl.ds(0, BATCH)], buf.at[slot], sem.at[slot]).wait()
    sub = buf.shape[2]
    per = D // LANES
    wide[...] = buf[slot].astype(jnp.float32).reshape(BATCH * sub, LANES)
    for j in range(per):
        out_ref[:, LANES * j : LANES * (j + 1)] = wide[
            pl.ds(j, BATCH * sub // per, stride=per), :
        ].astype(jnp.bfloat16)


def pad_index(index):
    count = index.shape[0]
    return jnp.pad(index, (0, pl.cdiv(count, BATCH) * BATCH - count)).astype(jnp.int32)


def unpack(streams, index):
    first, second = streams
    count = index.shape[0]
    sub = first.shape[1]
    rows = sub * LANES // D
    return pl.pallas_call(
        unpack_kernel,
        out_shape=jax.ShapeDtypeStruct((count * rows, D), jnp.bfloat16),
        grid_spec=pltpu.PrefetchScalarGridSpec(
            num_scalar_prefetch=1,
            grid=(pl.cdiv(count, BATCH),),
            in_specs=[pl.BlockSpec(memory_space=pl.ANY), pl.BlockSpec(memory_space=pl.ANY)],
            out_specs=pl.BlockSpec((BATCH * rows, D), lambda i, idx: (i, 0)),
            scratch_shapes=[
                pltpu.VMEM((2, BATCH, sub, LANES), jnp.bfloat16),
                pltpu.VMEM((BATCH * sub, LANES), jnp.float32),
                pltpu.SemaphoreType.DMA((2,)),
            ],
        ),
        cost_estimate=pl.CostEstimate(
            flops=0, bytes_accessed=4 * count * sub * LANES, transcendentals=0
        ),
        name="unpack",
    )(pad_index(index), first, second)


def own_kernel(limits, idx_ref, *refs):
    sources = refs[: len(limits)]
    out_ref, buf, sem = refs[len(limits) :]
    i = pl.program_id(0)
    slot = lax.rem(i, 2)

    def fetch(step, which):
        def body(k, carry):
            b = idx_ref[step * BATCH + k]
            start = 0
            for source, limit in zip(sources, limits):

                @pl.when((b >= start) & (b < start + limit))
                def _(source=source, start=start):
                    pltpu.make_async_copy(
                        source.at[b - start], buf.at[which, k], sem.at[which]
                    ).start()

                start += limit
            return carry

        lax.fori_loop(0, BATCH, body, 0, unroll=8)

    @pl.when(i == 0)
    def _():
        fetch(0, 0)

    @pl.when(i + 1 < pl.num_programs(0))
    def _():
        fetch(i + 1, 1 - slot)

    pltpu.make_async_copy(sources[0].at[pl.ds(0, BATCH)], buf.at[slot], sem.at[slot]).wait()
    out_ref[...] = buf[slot].astype(jnp.float32)


def take_blocks(streams, index, extra=0):
    count = index.shape[0]
    sub = streams[0].shape[1]
    return pl.pallas_call(
        functools.partial(own_kernel, tuple(s.shape[0] for s in streams)),
        out_shape=jax.ShapeDtypeStruct((count + extra, sub, LANES), jnp.float32),
        grid_spec=pltpu.PrefetchScalarGridSpec(
            num_scalar_prefetch=1,
            grid=(pl.cdiv(count, BATCH),),
            in_specs=[pl.BlockSpec(memory_space=pl.ANY)] * len(streams),
            out_specs=pl.BlockSpec((BATCH, sub, LANES), lambda i, idx: (i, 0, 0)),
            scratch_shapes=[
                pltpu.VMEM((2, BATCH, sub, LANES), jnp.bfloat16),
                pltpu.SemaphoreType.DMA((2,)),
            ],
        ),
        name="take_blocks",
    )(pad_index(index), *streams)


def pack_kernel(count, keep, idx_ref, src_ref, *refs):
    first_ref, second_ref, wide, buf, sem = refs[2:] if keep else refs
    i = pl.program_id(0)
    steps = pl.num_programs(0)
    slot = lax.rem(i, 2)
    limit = first_ref.shape[0]
    sub = buf.shape[2]
    per = D // LANES
    last = count - (pl.cdiv(count, BATCH) - 1) * BATCH

    def drain(which, blocks):
        pltpu.make_async_copy(
            buf.at[which, pl.ds(0, blocks)], first_ref.at[pl.ds(0, blocks)], sem.at[which]
        ).wait()

    @pl.when(i >= 2)
    def _():
        drain(slot, BATCH)

    for j in range(per):
        wide[pl.ds(j, BATCH * sub // per, stride=per), :] = src_ref[
            :, LANES * j : LANES * (j + 1)
        ].astype(jnp.float32)
    buf[slot] = wide[...].reshape(BATCH, sub, LANES).astype(jnp.bfloat16)

    def body(k, carry):
        b = idx_ref[i * BATCH + k]

        @pl.when(b < limit)
        def _():
            pltpu.make_async_copy(buf.at[slot, k], first_ref.at[b], sem.at[slot]).start()

        @pl.when(b >= limit)
        def _():
            pltpu.make_async_copy(buf.at[slot, k], second_ref.at[b - limit], sem.at[slot]).start()

        return carry

    @pl.when(i < steps - 1)
    def _():
        lax.fori_loop(0, BATCH, body, 0, unroll=8)

    @pl.when(i == steps - 1)
    def _():
        lax.fori_loop(0, last, body, 0)
        drain(slot, last)

        @pl.when(i >= 1)
        def _():
            drain(1 - slot, BATCH)


def pack(grad, index, size, streams=None):
    count = index.shape[0]
    rows = grad.shape[0] // count
    sub = rows * D // LANES
    keep = streams is not None
    shape = jax.ShapeDtypeStruct((size, sub, LANES), jnp.bfloat16)
    anywhere = pl.BlockSpec(memory_space=pl.ANY)
    return pl.pallas_call(
        functools.partial(pack_kernel, count, keep),
        out_shape=(shape, shape),
        grid_spec=pltpu.PrefetchScalarGridSpec(
            num_scalar_prefetch=1,
            grid=(pl.cdiv(count, BATCH),),
            in_specs=[pl.BlockSpec((BATCH * rows, D), lambda i, idx: (i, 0))]
            + ([anywhere, anywhere] if keep else []),
            out_specs=(anywhere, anywhere),
            scratch_shapes=[
                pltpu.VMEM((BATCH * sub, LANES), jnp.float32),
                pltpu.VMEM((2, BATCH, sub, LANES), jnp.bfloat16),
                pltpu.SemaphoreType.DMA((2,)),
            ],
        ),
        input_output_aliases={2: 0, 3: 1} if keep else {},
        cost_estimate=pl.CostEstimate(
            flops=0, bytes_accessed=6 * count * sub * LANES, transcendentals=0
        ),
        name="pack",
    )(pad_index(index), grad, *(streams if keep else ()))


def update_kernel(scal_ref, count_ref, grad_ref, m_ref, f_ref, s_ref, om_ref, of_ref, os_ref):
    i = pl.program_id(0)
    rows = grad_ref.shape[0]
    row = i * rows + lax.broadcasted_iota(jnp.int32, grad_ref.shape, 0)
    keep = row < count_ref[0]
    clipped = scal_ref[0] * grad_ref[...].astype(jnp.float32)
    master = m_ref[...]
    new_first = BETA_ONE * f_ref[...] + (1.0 - BETA_ONE) * clipped
    new_second = BETA_TWO * s_ref[...] + (1.0 - BETA_TWO) * clipped * clipped
    step_size = (
        new_first
        / (1.0 - BETA_ONE**ADAM_STEP)
        / (jnp.sqrt(new_second / (1.0 - BETA_TWO**ADAM_STEP)) + ADAM_EPS)
    )
    new_master = master - LEARN_RATE * (step_size + WEIGHT_DECAY * master)
    om_ref[...] = jnp.where(keep, new_master, 0.0)
    of_ref[...] = jnp.where(keep, new_first, 0.0)
    os_ref[...] = jnp.where(keep, new_second, 0.0)


def update(factor, valid, grad, master, first, second):
    count, sub, _ = grad.shape
    tile = next(t for t in range(64, 0, -1) if count % t == 0)
    spec = pl.BlockSpec((tile, sub, LANES), lambda i, a, b: (i, 0, 0))
    shape = jax.ShapeDtypeStruct(grad.shape, jnp.float32)
    return pl.pallas_call(
        update_kernel,
        out_shape=(shape, shape, shape),
        grid_spec=pltpu.PrefetchScalarGridSpec(
            num_scalar_prefetch=2,
            grid=(count // tile,),
            in_specs=[spec] * 4,
            out_specs=(spec, spec, spec),
        ),
        name="update",
    )(factor.reshape(1), valid.reshape(1), grad, master, first, second)


class Part:
    def __init__(self, lo, hi, chunk, member, before, counts_before, ring_pos, my_pos):
        groups = member.shape[1]
        self.lo, self.count, self.groups, self.chunk = lo, hi - lo, groups, chunk
        self.size = (hi - lo) // 2 + groups + (groups + 1) * chunk
        inside = member[lo:hi]
        self.held = jnp.sum(inside, axis=0)
        self.base = counts_before
        rank = jnp.sum((before[lo:hi] - counts_before[None, :]) * inside, axis=1)
        half = (self.held + 1) // 2
        halves = (half, self.held - half)
        self.half = half
        self.steps = []
        self.gather_seg, self.scatter_seg, self.lag, self.scatter_lag = [], [], [], []
        padded_sum = []
        steps = jnp.zeros((), jnp.int32)
        slots = jnp.arange(groups, dtype=jnp.int32)
        for way in (0, 1):
            wide = jnp.maximum(halves[way], chunk)
            at_ring = jnp.sum(jnp.where(ring_pos[None, :] == slots[:, None], wide[None, :], 0), axis=1)
            steps = jnp.maximum(steps, jnp.max(jnp.sum(at_ring) - at_ring))
            turn = 1 if way == 0 else -1

            def starts(origin):
                gap = ((origin - slots) * turn) % groups
                earlier = gap[None, :] < gap[:, None]
                return jnp.sum(jnp.where(earlier, at_ring[None, :], 0), axis=1)

            def by_group(ring_values):
                return jnp.sum(
                    jnp.where(ring_pos[:, None] == slots[None, :], ring_values[None, :], 0), axis=1
                )

            here = jnp.sum(jnp.where(slots == my_pos, at_ring, 0))
            prev = jnp.sum(jnp.where(slots == (my_pos - turn) % groups, at_ring, 0))
            self.lag.append(here)
            self.scatter_lag.append(prev)
            self.gather_seg.append(by_group(starts(my_pos)))
            self.scatter_seg.append(by_group(starts((my_pos - turn) % groups)))
        self.dyn_steps = (steps + chunk - 1) // chunk
        self.fixed_steps = pl.cdiv(int(0.46 * (hi - lo)), chunk)

        def place(seg):
            up = jnp.sum((seg[0])[None, :] * inside, axis=1) + rank
            down = jnp.sum((seg[1] - half)[None, :] * inside, axis=1) + rank + self.size
            return jnp.where(rank < jnp.sum(half[None, :] * inside, axis=1), up, down)

        self.gather_place = place(self.gather_seg)
        self.scatter_place = place(self.scatter_seg)


def ring_links(count):
    order = ring_order(count)
    up = [(order[k], order[(k + 1) % count]) for k in range(count)]
    return up, [(b, a) for a, b in up]


def pick(vector, index):
    return jnp.sum(jnp.where(jnp.arange(vector.shape[0]) == index, vector, 0))


def run_ring(part, streams, step):
    for s in range(part.fixed_steps):
        streams = [step(s, way, streams[way]) for way in (0, 1)]

    def body(s, carry):
        return tuple(step(s, way, carry[way]) for way in (0, 1))

    return lax.fori_loop(part.fixed_steps, part.dyn_steps, body, tuple(streams))


def ring_gather(part, own, group_index):
    links = ring_links(part.groups)
    base = pick(part.base, group_index)
    half = pick(part.half, group_index)
    streams = [
        lax.dynamic_slice_in_dim(own, start, part.size) for start in (base, base + half)
    ]

    def step(s, way, stream):
        sent = lax.dynamic_slice_in_dim(stream, s * part.chunk, part.chunk)
        got = lax.ppermute(sent, "grp", links[way])
        at = jnp.minimum(part.lag[way] + s * part.chunk, part.size - part.chunk)
        return lax.dynamic_update_slice_in_dim(stream, got, at, 0)

    return run_ring(part, streams, step)


def ring_scatter(part, streams):
    links = ring_links(part.groups)

    def step(s, way, stream):
        sent = lax.dynamic_slice_in_dim(stream, s * part.chunk, part.chunk)
        got = lax.ppermute(sent, "grp", links[way])
        at = jnp.minimum(part.scatter_lag[way] + s * part.chunk, part.size - part.chunk)
        old = lax.dynamic_slice_in_dim(stream, at, part.chunk)
        total = (old.astype(jnp.float32) + got.astype(jnp.float32)).astype(jnp.bfloat16)
        return lax.dynamic_update_slice_in_dim(stream, total, at, 0)

    return run_ring(part, streams, step)


def own_index(part, group_index, row, offset):
    k = row - pick(part.base, group_index)
    half = pick(part.half, group_index)
    up = pick(part.scatter_seg[0], group_index) + k
    down = pick(part.scatter_seg[1], group_index) + k - half + part.size
    inside = (k >= 0) & (k < pick(part.held, group_index))
    return inside, jnp.where(k < half, up, down) + offset


def sum_everywhere(values):
    values = jnp.zeros((8, LANES), jnp.float32).at[0, : values.shape[0]].set(values)
    for axis in ("ep", "grp"):
        size = lax.axis_size(axis)
        step = 1
        while step < size:
            pairs = [(k, k ^ step) for k in range(size)]
            values = values + lax.ppermute(values, axis, pairs)
            step *= 2
    return values[0, 0], values[0, 1]


def on_device(
    token_ids,
    expert_routes,
    route_weights,
    action_positions,
    action_tokens,
    advantages,
    value_targets,
    owners,
    master_weights,
    first_moment,
    second_moment,
):
    groups = lax.axis_size("grp")
    shards = lax.axis_size("ep")
    group_index = lax.axis_index("grp")
    shard_index = lax.axis_index("ep")
    capacity = master_weights.shape[0]
    row_width = master_weights.shape[2]
    blocks = owners.shape[0]
    length = token_ids.shape[2]
    act_count = action_positions.shape[2]
    local_experts = EXPERTS // shards
    vocab_rows = VOCAB // shards
    npos = groups * shards * act_count
    groups_per = HEADS // KV
    embed_scale = math.sqrt(D) / 2.0
    gu_size = local_experts * D * 2 * FF
    dn_size = local_experts * FF * D
    col_size = gu_size + dn_size + vocab_rows * D
    query_end = col_size + D * HEADS * HD
    keyval_end = query_end + D * 2 * KV * HD
    out_end = keyval_end + HEADS * HD * D
    sub = row_width // LANES
    order = ring_order(groups)
    ring_pos = jnp.array([order.index(g) for g in range(groups)], jnp.int32)
    my_pos = pick(ring_pos, group_index)
    member = (owners[:, None] == jnp.arange(groups, dtype=jnp.int32)[None, :]).astype(jnp.int32)
    before = jnp.cumsum(member, axis=0) - member
    marks = [0, (gu_size + dn_size) // row_width, col_size // row_width, blocks]
    chunks = [144, 144, 104]
    parts = []
    counts_before = jnp.zeros((groups,), jnp.int32)
    for lo, hi, chunk in zip(marks[:-1], marks[1:], chunks):
        parts.append(Part(lo, hi, chunk, member, before, counts_before, ring_pos, my_pos))
        counts_before = counts_before + parts[-1].held
    exp_part, tab_part, att_part = parts
    master_rows = master_weights.reshape(capacity, sub, LANES)
    own = cast_rows(master_rows, max(part.size for part in parts))
    att_streams = ring_gather(att_part, own, group_index)
    own_next, att_streams = lax.optimization_barrier((own, att_streams))
    exp_streams = ring_gather(exp_part, own_next, group_index)
    own_next, exp_streams = lax.optimization_barrier((own_next, exp_streams))
    tab_streams = ring_gather(tab_part, own_next, group_index)
    table = unpack(tab_streams, tab_part.gather_place)
    gu_nb = gu_size // row_width
    gate_up = unpack(exp_streams, exp_part.gather_place[:gu_nb]).reshape(local_experts, D, 2 * FF)
    down = unpack(exp_streams, exp_part.gather_place[gu_nb:]).reshape(local_experts, FF, D)
    q_nb = (query_end - col_size) // row_width
    kv_nb = (keyval_end - col_size) // row_width
    o_nb = (out_end - col_size) // row_width
    att_place = att_part.gather_place
    w_query = unpack(att_streams, att_place[:q_nb])
    w_keyval = unpack(att_streams, att_place[q_nb:kv_nb])
    w_out = unpack(att_streams, att_place[kv_nb:o_nb])
    gains = unpack(att_streams, att_place[o_nb:])[: 4].astype(jnp.float32)
    group_ids = token_ids.reshape(shards * length)
    local_ids = group_ids - shard_index * vocab_rows
    inside = (local_ids >= 0) & (local_ids < vocab_rows)
    order_ids = jnp.arange(shards * length, dtype=jnp.int32)
    same = group_ids[:, None] == group_ids[None, :]
    first = ~jnp.any(same & (order_ids[None, :] < order_ids[:, None]), axis=1)
    shard_of = group_ids // vocab_rows
    most = jnp.max(
        jnp.sum(
            (first[:, None] & (shard_of[:, None] == jnp.arange(shards)[None, :])).astype(jnp.int32),
            axis=0,
        )
    )
    own_first = (first & inside).astype(jnp.int32)
    first_slot = jnp.cumsum(own_first) - own_first
    token_slot = jnp.sum(jnp.where(same & (own_first[None, :] > 0), first_slot[None, :], 0), axis=1)
    token_slot = jnp.where(inside, token_slot, -1)
    most = jnp.max(lax.all_gather(most.reshape(1), "grp", axis=0))
    rounds = (most + FRESH - 1) // FRESH
    tab_rank = jnp.sum(
        jnp.where(
            jnp.arange(groups, dtype=jnp.int32)[None, :] == group_index,
            jnp.where(member > 0, before, -1),
            0,
        ),
        axis=1,
    )[marks[1] : marks[2]]
    rows_a_block = row_width // D
    row_tile = D // LANES
    own_rows = own.reshape(own.shape[0] * rows_a_block, row_tile, LANES)
    slot_range = jnp.arange(FRESH, dtype=jnp.int32)

    def wanted(turn):
        mine = (own_first[None, :] > 0) & (
            first_slot[None, :] == (turn * FRESH + slot_range)[:, None]
        )
        listed = jnp.sum(jnp.where(mine, local_ids[None, :] + 1, 0), axis=1) - 1
        listed = lax.all_gather(listed, "grp", axis=0)
        rank = tab_rank[jnp.maximum(listed, 0) // rows_a_block]
        here = (listed >= 0) & (rank >= 0)
        return jnp.where(here, rank * rows_a_block + listed % rows_a_block, -1)

    def spread(turn):
        return (
            token_slot[:, None] == (turn * FRESH + slot_range)[None, :]
        ).astype(jnp.bfloat16)

    def shifted(shift):
        return [(g, (g + shift) % groups) for g in range(groups)]

    def fresh_rows(turn, want):
        flat = want.reshape(-1)
        supply = jnp.where(
            (flat >= 0)[:, None, None], own_rows[jnp.maximum(flat, 0)], jnp.zeros((), jnp.bfloat16)
        ).reshape(groups, FRESH, row_tile, LANES)
        rows_now = lax.dynamic_index_in_dim(supply, group_index, 0, keepdims=False)
        for shift in range(1, groups):
            away = lax.dynamic_index_in_dim(
                supply, (group_index + shift) % groups, 0, keepdims=False
            )
            rows_now = rows_now + lax.ppermute(away, "grp", shifted(shift))
        return jnp.dot(
            spread(turn), rows_now.reshape(FRESH, D), preferred_element_type=jnp.float32
        ).astype(jnp.bfloat16)

    want_now = wanted(0)
    found = fresh_rows(0, want_now)
    found = lax.fori_loop(
        1, rounds, lambda turn, so_far: so_far + fresh_rows(turn, wanted(turn)), found
    )
    x_embed = embed_scale * lax.psum_scatter(found, "ep", scatter_dimension=0, tiled=True).astype(
        jnp.float32
    )
    places = action_positions.reshape(act_count)
    cosine, sine_table = rope_tables(length)
    score_scale = HD ** (-0.5)
    rows = length
    slots = CAP_EXP
    causal = jnp.arange(length)[:, None] >= jnp.arange(length)[None, :]
    sum_type = jnp.bfloat16

    def take(values):
        return values

    def put(values):
        return values

    cosine_q, sine_q = take(cosine), take(sine_table)
    routing = jnp.concatenate(
        [
            take(expert_routes.reshape(length, TOP)).astype(jnp.float32),
            take(route_weights.reshape(length, TOP)),
        ],
        axis=1,
    )
    routing = lax.all_gather(routing, "ep", axis=0)
    local_ids_exp = shard_index * local_experts + jnp.arange(local_experts, dtype=jnp.int32)
    named = routing[:, :, None, :TOP] == local_ids_exp[None, None, :, None].astype(jnp.float32)
    routed = jnp.sum(named.astype(jnp.float32), axis=3)
    pair_weight = jnp.sum(jnp.where(named, routing[:, :, None, TOP:], 0.0), axis=3)
    earlier_row = (jnp.arange(rows)[:, None] < jnp.arange(rows)[None, :]).astype(jnp.bfloat16)
    slot_of = jnp.einsum(
        "pt,spj->sjt",
        earlier_row,
        routed.astype(jnp.bfloat16),
        preferred_element_type=jnp.float32,
    )
    slot_of = jnp.where(jnp.swapaxes(routed, 1, 2) > 0.0, slot_of, -1.0)
    held = slot_of[:, :, None, :] == jnp.arange(slots, dtype=jnp.float32)[None, None, :, None]
    dealt = held.astype(jnp.bfloat16)
    slot_weight = jnp.sum(
        jnp.where(held, jnp.swapaxes(pair_weight, 1, 2)[:, :, None, :], 0.0), axis=3
    )[..., None]

    def to_experts(values):
        return jnp.einsum("sjcp,spd->sjcd", dealt, values, preferred_element_type=jnp.float32)

    def from_experts(values):
        partial = jnp.einsum(
            "sjcp,sjcd->spd", dealt, values, preferred_element_type=jnp.float32
        ).astype(sum_type)
        return lax.psum_scatter(
            partial.reshape(shards * rows, D), "ep", scatter_dimension=0, tiled=True
        ).astype(jnp.float32)

    normed = rms_norm(x_embed, gains[0]).astype(jnp.bfloat16)
    normed_q = take(normed)
    query = jnp.dot(normed_q, w_query, preferred_element_type=jnp.float32).reshape(rows, HEADS, HD)
    keyval = jnp.dot(normed, w_keyval, preferred_element_type=jnp.float32).reshape(
        length, 2, KV, HD
    )
    query_low = rotate(query, cosine_q, sine_q).astype(jnp.bfloat16)
    query_low = query_low.reshape(rows, KV, groups_per, HD)
    keys_low = rotate(keyval[:, 0], cosine, sine_table).astype(jnp.bfloat16)
    values_low = keyval[:, 1].astype(jnp.bfloat16)

    def score_block():
        scores = (
            jnp.einsum("tkgd,skd->kgts", query_low, keys_low, preferred_element_type=jnp.float32)
            * score_scale
        )
        return jnp.where(causal, scores, MASK_FILL)

    scores = score_block()
    peak_score = jnp.max(scores, axis=-1, keepdims=True)
    expo = jnp.exp(scores - peak_score)
    denom = jnp.sum(expo, axis=-1, keepdims=True)
    log_denom = peak_score + jnp.log(denom)
    probs_low = (expo / denom).astype(jnp.bfloat16)
    attended = jnp.einsum(
        "kgts,skd->tkgd", probs_low, values_low, preferred_element_type=jnp.float32
    )
    attended = attended.reshape(rows, HEADS * HD).astype(jnp.bfloat16)
    x_attn = take(x_embed) + jnp.dot(attended, w_out, preferred_element_type=jnp.float32)
    mixed = rms_norm(x_attn, gains[1]).astype(jnp.bfloat16)
    mixed_all = lax.all_gather(mixed, "ep", axis=0)
    arrived = to_experts(mixed_all).astype(jnp.bfloat16)
    gate_val = jnp.einsum("sjcd,jdf->sjcf", arrived, gate_up, preferred_element_type=jnp.float32)
    gate_part = gate_val[..., :FF]
    up_part = gate_val[..., FF:]
    sigma = jax.nn.sigmoid(gate_part)
    hidden = (gate_part * sigma * up_part).astype(jnp.bfloat16)
    produced = jnp.einsum(
        "sjcf,jfd->sjcd", hidden, down, preferred_element_type=jnp.float32
    ).astype(jnp.bfloat16)
    weighted = (slot_weight * produced.astype(jnp.float32)).astype(jnp.bfloat16)
    x_final = x_attn + from_experts(weighted)
    final = rms_norm(x_final, gains[2])
    picked = final[places]
    value_pred = jnp.dot(picked, gains[3], precision=lax.Precision.HIGHEST)
    group_rows = lax.all_gather(picked.astype(jnp.bfloat16), "ep", axis=0, tiled=True)
    logits = jnp.einsum("ad,vd->av", group_rows, table, preferred_element_type=jnp.float32)
    targets = action_tokens.reshape(shards * act_count) - shard_index * vocab_rows
    target_mask = jnp.arange(vocab_rows, dtype=jnp.int32)[None, :] == targets[:, None]
    target_logit = jnp.sum(jnp.where(target_mask, logits, 0.0), axis=1)
    local_peak = jnp.max(logits, axis=1)
    local_mass = jnp.sum(jnp.exp(logits - local_peak[:, None]), axis=1)
    stats = lax.all_gather(jnp.stack([local_peak, local_mass, target_logit]), "ep", axis=0)
    all_peak = jnp.max(stats[:, 0], axis=0)
    all_mass = jnp.sum(stats[:, 1] * jnp.exp(stats[:, 0] - all_peak[None, :]), axis=0)
    all_target = jnp.sum(stats[:, 2], axis=0)
    log_norm = all_peak + jnp.log(all_mass)
    logp = all_target - log_norm
    group_adv = advantages.reshape(shards * act_count)
    own_logp = lax.dynamic_slice_in_dim(logp, shard_index * act_count, act_count)
    own_adv = lax.dynamic_slice_in_dim(group_adv, shard_index * act_count, act_count)
    own_targets = value_targets.reshape(act_count)
    local_loss = jnp.sum(-own_adv * own_logp + VALUE_COEF * (value_pred - own_targets) ** 2)
    soft = jnp.exp(logits - log_norm[:, None])
    d_logits = ((group_adv / npos)[:, None] * (soft - target_mask.astype(jnp.float32))).astype(
        jnp.bfloat16
    )
    grad_table = jnp.einsum("av,ad->vd", d_logits, group_rows, preferred_element_type=jnp.float32)
    tab_sums = ring_scatter(tab_part, pack(grad_table, tab_part.scatter_place, tab_part.size))
    head_part = jnp.einsum("av,vd->ad", d_logits, table, preferred_element_type=jnp.float32)
    grad_picked = lax.psum_scatter(head_part, "ep", scatter_dimension=0, tiled=True)
    grad_value = 2.0 * VALUE_COEF * (value_pred - own_targets) / npos
    grad_picked = grad_picked + grad_value[:, None] * gains[3][None, :]
    grad_vhead = jnp.dot(grad_value, picked, precision=lax.Precision.HIGHEST)
    grad_final = jnp.zeros((length, D), jnp.float32).at[places].add(grad_picked)
    _, final_back = jax.vjp(rms_norm, x_final, gains[2])
    grad_x_final, grad_gain_two = final_back(grad_final)
    grad_final_all = lax.all_gather(grad_x_final.astype(jnp.bfloat16), "ep", axis=0)
    grad_arrived = (slot_weight * to_experts(grad_final_all)).astype(jnp.bfloat16)
    grad_down = jnp.einsum(
        "sjcf,sjcd->jfd", hidden, grad_arrived, preferred_element_type=jnp.float32
    )
    grad_hidden = jnp.einsum(
        "sjcd,jfd->sjcf", grad_arrived, down, preferred_element_type=jnp.float32
    )
    grad_gate = grad_hidden * up_part * sigma * (1.0 + gate_part * (1.0 - sigma))
    grad_up = grad_hidden * gate_part * sigma
    grad_gate_val = jnp.concatenate([grad_gate, grad_up], axis=-1).astype(jnp.bfloat16)
    grad_gate_up = jnp.einsum(
        "sjcd,sjcf->jdf", arrived, grad_gate_val, preferred_element_type=jnp.float32
    )
    grad_inputs = jnp.einsum(
        "sjcf,jdf->sjcd", grad_gate_val, gate_up, preferred_element_type=jnp.float32
    ).astype(jnp.bfloat16)
    grad_mixed = from_experts(grad_inputs)
    _, mixed_back = jax.vjp(rms_norm, x_attn, gains[1])
    grad_norm_in, grad_gain_one = mixed_back(grad_mixed)
    grad_x_attn = grad_x_final + grad_norm_in
    grad_attn_low = grad_x_attn.astype(jnp.bfloat16)
    grad_attended = jnp.einsum(
        "td,id->ti", grad_attn_low, w_out, preferred_element_type=jnp.float32
    )
    grad_attended = grad_attended.astype(jnp.bfloat16).reshape(rows, KV, groups_per, HD)
    probs = jnp.exp(score_block() - log_denom)
    probs_again = probs.astype(jnp.bfloat16)
    grad_values = jnp.einsum(
        "kgts,tkgd->skd", probs_again, grad_attended, preferred_element_type=jnp.float32
    )
    grad_probs = jnp.einsum(
        "tkgd,skd->kgts", grad_attended, values_low, preferred_element_type=jnp.float32
    )
    row_delta = jnp.sum(grad_probs * probs, axis=-1, keepdims=True)
    grad_scores = (probs * (grad_probs - row_delta)).astype(jnp.bfloat16)
    grad_query = (
        jnp.einsum("kgts,skd->tkgd", grad_scores, keys_low, preferred_element_type=jnp.float32)
        * score_scale
    )
    grad_keys = (
        jnp.einsum("kgts,tkgd->skd", grad_scores, query_low, preferred_element_type=jnp.float32)
        * score_scale
    )
    grad_query = (
        rotate_back(grad_query.reshape(rows, HEADS, HD), cosine_q, sine_q)
        .reshape(rows, HEADS * HD)
        .astype(jnp.bfloat16)
    )
    grad_keys = rotate_back(grad_keys, cosine, sine_table)
    grad_keyval = (
        jnp.stack([grad_keys, grad_values], axis=1)
        .reshape(length, 2 * KV * HD)
        .astype(jnp.bfloat16)
    )
    grad_normed = put(
        jnp.einsum("ti,di->td", grad_query, w_query, preferred_element_type=jnp.float32)
    ) + jnp.einsum("ti,di->td", grad_keyval, w_keyval, preferred_element_type=jnp.float32)
    _, embed_back = jax.vjp(rms_norm, x_embed, gains[0])
    grad_norm_embed, grad_gain_zero = embed_back(grad_normed)
    grad_rows = (embed_scale * (put(grad_x_attn) + grad_norm_embed)).astype(jnp.bfloat16)
    grad_gains = jnp.stack([grad_gain_zero, grad_gain_one, grad_gain_two, grad_vhead])
    gains_high = grad_gains.astype(jnp.bfloat16)
    gains_low = (grad_gains - gains_high.astype(jnp.float32)).astype(jnp.bfloat16)
    ahead = lax.all_gather(jnp.concatenate([attended, normed_q, normed], axis=0), "ep", axis=0)
    behind = lax.all_gather(
        jnp.concatenate(
            [grad_attn_low, grad_query, grad_keyval, grad_rows, gains_high, gains_low], axis=0
        ),
        "ep",
        axis=0,
    )

    def outer(ins, outs):
        return jnp.einsum("sti,sto->io", ins, outs, preferred_element_type=jnp.float32)

    grad_w_out = outer(ahead[:, :rows], behind[:, :rows])
    grad_w_query = outer(ahead[:, rows : 2 * rows], behind[:, rows : 2 * rows])
    grad_w_keyval = outer(ahead[:, 2 * rows :], behind[:, 2 * rows : 2 * rows + length])
    all_rows = behind[:, 2 * rows + length : 2 * (rows + length)].reshape(shards * length, D)
    grad_gains = jnp.sum(
        behind[:, 2 * (rows + length) :].astype(jnp.float32).reshape(shards, 2, 4, D),
        axis=(0, 1),
    )
    att_grads = (grad_w_query, grad_w_keyval, grad_w_out, grad_gains)
    att_rows = jnp.concatenate([piece.reshape(-1, D) for piece in att_grads], axis=0)
    exp_sums = pack(grad_gate_up.reshape(-1, D), exp_part.scatter_place[:gu_nb], exp_part.size)
    exp_sums = pack(
        grad_down.reshape(-1, D), exp_part.scatter_place[gu_nb:], exp_part.size, exp_sums
    )
    tab_sums, exp_sums = lax.optimization_barrier((tab_sums, exp_sums))
    exp_sums = ring_scatter(exp_part, exp_sums)
    row = jnp.arange(capacity, dtype=jnp.int32)
    valid = pick(counts_before, group_index)
    own_col = pick(att_part.base, group_index)
    in_exp, place = own_index(exp_part, group_index, row, 0)
    in_tab, tab_place = own_index(tab_part, group_index, row, 2 * exp_part.size)
    place = jnp.where(in_exp, place, jnp.where(in_tab, tab_place, 0))
    owned = take_blocks((*exp_sums, *tab_sums), place, att_part.count)

    def add_fresh(turn, want, so_far):
        sums = jnp.einsum(
            "nk,nd->kd", spread(turn), all_rows, preferred_element_type=jnp.float32
        ).astype(jnp.bfloat16)
        sums = sums.reshape(FRESH, row_tile, LANES)
        gone = so_far.shape[0]
        for shift in range(groups):
            came = lax.ppermute(sums, "grp", shifted(shift)) if shift else sums
            at = lax.dynamic_index_in_dim(
                want, (group_index - shift) % groups, 0, keepdims=False
            )
            so_far = so_far.at[jnp.where(at >= 0, at, gone)].add(
                came.astype(jnp.float32), mode="drop"
            )
        return so_far

    owned_rows = owned.reshape(owned.shape[0] * rows_a_block, row_tile, LANES)
    owned_rows = add_fresh(0, want_now, owned_rows)
    owned_rows = lax.fori_loop(
        1, rounds, lambda turn, so_far: add_fresh(turn, wanted(turn), so_far), owned_rows
    )
    owned = owned_rows.reshape(owned.shape)
    exp_sums, att_grad_streams = lax.optimization_barrier(
        (exp_sums, pack(att_rows, att_part.scatter_place, att_part.size))
    )
    att_sums = ring_scatter(att_part, att_grad_streams)
    _, att_place = own_index(
        att_part, group_index, own_col + jnp.arange(att_part.count, dtype=jnp.int32), 0
    )
    att_place = jnp.clip(att_place, 0, 2 * att_part.size - 1)
    owned = lax.dynamic_update_slice_in_dim(owned, take_blocks(att_sums, att_place), own_col, 0)
    filled = row < valid
    owned = owned[:capacity]
    counted = (filled & ((row < own_col) | (shard_index == 0))).reshape(capacity, 1, 1)
    wide_owned = owned.astype(jnp.float32)
    square = jnp.sum(jnp.where(counted, wide_owned * wide_owned, 0.0))
    square_all, loss_all = sum_everywhere(jnp.stack([square, local_loss]))
    grad_norm = jnp.sqrt(square_all)
    factor = jnp.minimum(1.0, CLIP_BASE / math.sqrt(npos) / grad_norm)
    outs = update(
        factor,
        valid,
        owned,
        master_rows,
        first_moment.reshape(capacity, sub, LANES),
        second_moment.reshape(capacity, sub, LANES),
    )
    return (loss_all / npos, grad_norm) + tuple(o.reshape(master_weights.shape) for o in outs)


def solution(mesh):
    placed = (
        P("grp", None, None),
        P("grp", "ep", None, None),
        P("grp", "ep", None, None),
        P("grp", "ep", None),
        P("grp", None, None),
        P("grp", None, None),
        P("grp", "ep", None),
        P(),
        P("grp", "ep", None),
        P("grp", "ep", None),
        P("grp", "ep", None),
    )
    return jax.shard_map(
        on_device,
        mesh=mesh,
        in_specs=placed,
        out_specs=(P(), P(), P("grp", "ep", None), P("grp", "ep", None), P("grp", "ep", None)),
        check_vma=False,
    )
```
